256 devices in a mesh: seq: 16 (over z, x_hi), res: 16 (over x_lo, y, core).
Axes of the slice: x: 4 (x_hi: 2, x_lo: 2; x = x_hi * 2 + x_lo), y: 4, z: 8, core: 2. Of those that a mesh axis runs over, the one named last changes fastest.
Arguments:
- alignment: bfloat16 [256, 1024, 256], P('res', 'seq'), may hold values from -6 to 6
- alignment_mask: int32 [256, 1024], P('res', 'seq'), may hold values from 0 to 1, as said below
- residue_mask: int32 [1024], replicated, may hold values from 0 to 1, as said below
- pair_input: float32 [1024, 1024, 128], P('seq', 'res'), may hold values from -6 to 6
- outer_gain: float32 [256], replicated, may hold values from 0.25 to 1.75
- left_weight: bfloat16 [256, 32], replicated, may hold values from -0.375 to 0.375
- right_weight: bfloat16 [256, 32], replicated, may hold values from -0.375 to 0.375
- outer_weight: bfloat16 [1024, 128], replicated, may hold values from -1 to 1
- pair_gain: float32 [128], replicated, may hold values from 0.25 to 1.75
- bias_weight: bfloat16 [128, 8], replicated, may hold values from -48 to 48
- row_gain: float32 [256], replicated, may hold values from 0.25 to 1.75
- query_weight: bfloat16 [256, 256], replicated, may hold values from -0.375 to 0.375
- key_weight: bfloat16 [256, 256], replicated, may hold values from -0.375 to 0.375
- value_weight: bfloat16 [256, 256], replicated, may hold values from -0.375 to 0.375
- gate_weight: bfloat16 [256, 256], replicated, may hold values from -0.375 to 0.375
- output_weight: bfloat16 [256, 256], replicated, may hold values from -2 to 2
- transition_gain: float32 [256], replicated, may hold values from 0.25 to 1.75
- up_weight: bfloat16 [256, 1024], replicated, may hold values from -0.375 to 0.375
- down_weight: bfloat16 [1024, 256], replicated, may hold values from -0.1875 to 0.1875
Outputs:
- pair_output: float32 [1024, 1024, 128], P('seq', 'res')
- alignment_output: float32 [256, 1024, 256], P('res', 'seq')
The draws below stay inside these ranges and needn't reach their ends.
Inputs may be any that keep to these rules, and one draw needn't show every extreme that they name: `residue_mask`: 1 for a present residue, 0 for padding; at least one residue is 1 and at least one is 0. Some residue whose residue_mask is 1 has alignment_mask 1 in every sequence.
All inputs are finite; a program needn't handle non-finite values.
Results may differ from the reference program's by a relative error of at most 0.04.
Values may be sent and summed in bfloat16 or wider, within the bound.
A program may use at most 128 MiB of HBM per device.

```python
import math
import jax
import jax.numpy as jnp
from jax import lax

C_M = 256
C_Z = 128
HEADS = 8
HEAD = 32
OPM = 32
FF = 1024
SEQS = 256
RES = 1024


def mask_draws(key):
    base_key = jax.random.fold_in(key, 7001)
    mask_key, row_key, anchor_key, gap_key = jax.random.split(base_key, 4)
    anchor = jax.random.randint(anchor_key, (), 0, RES)
    gap = (anchor + 1 + jax.random.randint(gap_key, (), 0, RES - 1)) % RES
    positions = jnp.arange(RES)
    residue_draw = (jax.random.randint(mask_key, (RES,), 0, 8) > 0).astype(jnp.int32)
    residue_draw = jnp.where(positions == gap, 0, residue_draw)
    residue_draw = jnp.where(positions == anchor, 1, residue_draw)
    alignment_draw = (jax.random.randint(row_key, (SEQS, RES), 0, 4) > 0).astype(jnp.int32)
    alignment_draw = jnp.where(positions[None, :] == anchor, 1, alignment_draw)
    return (residue_draw, alignment_draw)


def draw_residue_mask(key, part):
    return mask_draws(key)[0]


def draw_alignment_mask(key, part):
    return mask_draws(key)[1]


def draw_bias_weight(key, part):
    base_key = jax.random.fold_in(key, 7003)
    normal_key = jax.random.fold_in(base_key, 0)
    weight = jax.random.normal(normal_key, (C_Z, HEADS), jnp.float32) * C_Z ** (-0.5)
    return jnp.clip(weight, -48.0, 48.0).astype(jnp.bfloat16)


def level_of(key, shape, shards, low, largest):
    gain, own = 1.0, jax.random.fold_in(key, 6)
    for axis_at, shards_of in shards:
        heights = jnp.exp(jax.random.uniform(jax.random.fold_in(own, axis_at), (shards_of,), jnp.float32, low / len(shards), largest / len(shards)))
        gain = gain * jnp.repeat(heights, shape[axis_at] // shards_of).reshape([-1 if axis == axis_at else 1 for axis in range(len(shape))])
    return gain


def scatter_about(own_key, dims, scale, bound, pieces=(), kind=jnp.bfloat16):
    values = jax.random.normal(own_key, dims, jnp.float32) * scale
    if len(pieces) > 0:
        values = level_of(own_key, dims, pieces, -0.22, 0.18) * values
    return jnp.clip(values, min=-bound, max=bound).astype(kind)


def setup_inputs(seed: int = 0) -> dict:
    arg_keys = jax.random.split(jax.random.key(seed), 20)
    return {
        "alignment": scatter_about(arg_keys[0], (SEQS, RES, C_M), 1.0, 6.0, ((0, 16), (1, 16))),
        "alignment_mask": draw_alignment_mask(jax.random.fold_in(arg_keys[19], 71), 0),
        "residue_mask": draw_residue_mask(jax.random.fold_in(arg_keys[19], 71), 0),
        "pair_input": scatter_about(arg_keys[3], (RES, RES, C_Z), 1.0, 6.0, ((0, 16), (1, 16)), jnp.float32),
        "outer_gain": jnp.clip(1.0 + 0.15 * jax.random.normal(arg_keys[4], (C_M,), jnp.float32), 0.25, 1.75),
        "left_weight": scatter_about(arg_keys[5], (C_M, OPM), C_M ** -0.5, 0.375),
        "right_weight": scatter_about(arg_keys[6], (C_M, OPM), C_M ** -0.5, 0.375),
        "outer_weight": scatter_about(arg_keys[7], (OPM * OPM, C_Z), OPM ** -0.5, 1.0),
        "pair_gain": jnp.clip(1.0 + 0.15 * jax.random.normal(arg_keys[8], (C_Z,), jnp.float32), 0.25, 1.75),
        "bias_weight": draw_bias_weight(jax.random.fold_in(arg_keys[19], 71), 0),
        "row_gain": jnp.clip(1.0 + 0.15 * jax.random.normal(arg_keys[10], (C_M,), jnp.float32), 0.25, 1.75),
        "query_weight": scatter_about(arg_keys[11], (C_M, HEADS * HEAD), C_M ** -0.5, 0.375),
        "key_weight": scatter_about(arg_keys[12], (C_M, HEADS * HEAD), C_M ** -0.5, 0.375),
        "value_weight": scatter_about(arg_keys[13], (C_M, HEADS * HEAD), C_M ** -0.5, 0.375),
        "gate_weight": scatter_about(arg_keys[14], (C_M, HEADS * HEAD), C_M ** -0.5, 0.375),
        "output_weight": scatter_about(arg_keys[15], (HEADS * HEAD, C_M), (HEAD // 4) ** -0.5, 2.0),
        "transition_gain": jnp.clip(1.0 + 0.15 * jax.random.normal(arg_keys[16], (C_M,), jnp.float32), 0.25, 1.75),
        "up_weight": scatter_about(arg_keys[17], (C_M, FF), C_M ** -0.5, 0.375),
        "down_weight": scatter_about(arg_keys[18], (FF, C_M), FF ** -0.5, 0.1875),
    }


EPSILON = 1e-05
MASKED = -1000000000.0

def layer_norm(values, scales):
    values = values.astype(jnp.float32)
    center = values - lax.optimization_barrier(jnp.mean(values, -1, keepdims=True))
    spread = lax.optimization_barrier(jnp.mean(center * center, -1, keepdims=True))
    return center * lax.rsqrt(spread + EPSILON) * scales

def project(values, weight):
    flattened = values.reshape(-1, values.shape[-1])
    result = jnp.dot(flattened, weight, preferred_element_type=jnp.float32)
    return result.reshape(values.shape[:-1] + (weight.shape[1],))

def reference(alignment, alignment_mask, residue_mask, pair_input, outer_gain, left_weight, right_weight, outer_weight, pair_gain, bias_weight, row_gain, query_weight, key_weight, value_weight, gate_weight, output_weight, transition_gain, up_weight, down_weight):
    live_mask = (alignment_mask * residue_mask[None, :]).astype(jnp.float32)
    outer_norm = layer_norm(alignment, outer_gain).astype(jnp.bfloat16)
    left_proj = (project(outer_norm, left_weight) * live_mask[..., None]).astype(jnp.bfloat16)
    right_proj = (project(outer_norm, right_weight) * live_mask[..., None]).astype(jnp.bfloat16)
    row_block = math.gcd(RES, 16)

    def outer_rows(row_start):
        left_piece = lax.dynamic_slice_in_dim(left_proj, row_start, row_block, 1).astype(jnp.float32)
        product = jnp.einsum('sic,sje->ijce', left_piece, right_proj.astype(jnp.float32)).astype(jnp.bfloat16)
        update = jnp.dot(product.reshape(row_block * RES, OPM * OPM), outer_weight, preferred_element_type=jnp.float32).reshape(row_block, RES, C_Z)
        live_rows = lax.dynamic_slice_in_dim(live_mask, row_start, row_block, 1)
        counts = jnp.einsum('si,sj->ij', live_rows, live_mask)
        return update / jnp.maximum(counts, 1.0)[..., None]
    starts = jnp.arange(RES // row_block, dtype=jnp.int32) * row_block
    outer_update = lax.map(outer_rows, starts).reshape(RES, RES, C_Z)
    pair_output = pair_input + outer_update
    pair_norm = layer_norm(pair_output, pair_gain).astype(jnp.bfloat16)
    pair_bias = project(pair_norm, bias_weight).astype(jnp.bfloat16)
    head_bias = jnp.transpose(pair_bias, (2, 0, 1)).astype(jnp.float32)
    row_norm = layer_norm(alignment, row_gain).astype(jnp.bfloat16)
    query_proj = project(row_norm, query_weight).astype(jnp.bfloat16)
    key_proj = project(row_norm, key_weight).astype(jnp.bfloat16)
    value_proj = project(row_norm, value_weight).astype(jnp.bfloat16)
    gate_values = jax.nn.sigmoid(project(row_norm, gate_weight))
    score_scale = HEAD ** (-0.5)

    def attend(inputs):
        query_row, key_row, value_row, live_row = inputs
        query_heads = query_row.astype(jnp.float32).reshape(RES, HEADS, HEAD)
        key_heads = key_row.astype(jnp.float32).reshape(RES, HEADS, HEAD)
        value_heads = value_row.astype(jnp.float32).reshape(RES, HEADS, HEAD)
        scores = jnp.einsum('ihd,jhd->hij', query_heads, key_heads) * score_scale + head_bias
        scores = jnp.where(live_row[None, None, :] > 0, scores, MASKED)
        score_peaks = lax.optimization_barrier(jnp.max(scores, -1, keepdims=True))
        weights = jnp.exp(scores - score_peaks)
        totals = lax.optimization_barrier(jnp.sum(weights, -1))
        rounded = lax.optimization_barrier(weights.astype(jnp.bfloat16)).astype(jnp.float32)
        mixed_sum = jnp.einsum('hij,jhd->ihd', rounded, value_heads)
        return (mixed_sum / jnp.transpose(totals)[..., None]).reshape(RES, HEADS * HEAD)
    attended = lax.map(attend, (query_proj, key_proj, value_proj, live_mask))
    gated_rows = (attended * gate_values).astype(jnp.bfloat16)
    after_rows = alignment.astype(jnp.float32) + project(gated_rows, output_weight)
    trans_norm = layer_norm(after_rows, transition_gain).astype(jnp.bfloat16)
    hidden_units = jnp.maximum(project(trans_norm, up_weight), 0.0).astype(jnp.bfloat16)
    alignment_output = after_rows + project(hidden_units, down_weight)
    return (pair_output, alignment_output)
```

```python
import functools

import jax
import jax.numpy as jnp
from jax import lax
from jax.experimental import pallas as pl
from jax.experimental.pallas import tpu as pltpu
from jax.sharding import PartitionSpec as P

EPSILON = 1e-05
MASKED = -1000000000.0
MESH = pl.DeviceIdType.MESH
F32, BF16 = jnp.float32, jnp.bfloat16
NN = (((1,), (0,)), ((), ()))
NT = (((1,), (1,)), ((), ()))
NZ = 8
HOPS = ((4, 3), (3, 4))


def mm(a, b, dims=NN):
    return lax.dot_general(a, b, dims, preferred_element_type=F32)


def kernel(
    left_in, right_in, kv_in, pair_in, align_in, w_ec, wb_t, pair_gain, wq, wg, wk, wv, wo, t_gain, w_up, w_down,
    expand, head_mask,
    pair_out, align_out,
    lg, rg, rt, bd, osc, inv_c, bias_own, bias_sib, bias_tab, kvg, kb, vb, mask_tab, sc_buf, p_buf, r_buf, tot_buf,
    gate_own, gate_far, gate_in,
    l_send, l_recv, t_sem, rx_sem, kx_sem, r_send, r_recv, k_send, k_recv, b_sem, pl_send, pl_recv, f_send, f_recv, g_sem,
):
    q = lax.axis_index("seq")
    r = lax.axis_index("res")
    z, x_hi = q // 2, q % 2
    core = r % 2
    y = (r // 2) % 4
    x_lo = r // 8
    x = x_hi * 2 + x_lo
    kt = r // 2
    mate_q = q + 1 - 2 * x_hi
    sib_r = r + 1 - 2 * core
    up_q = ((z + 1) % NZ) * 2 + x_hi
    down_q = ((z + NZ - 1) % NZ) * 2 + x_hi

    def dev(qq, rr):
        return {"seq": qq, "res": rr}

    def rcopy(src, dst, ss, rs, where):
        return pltpu.make_async_remote_copy(
            src_ref=src, dst_ref=dst, send_sem=ss, recv_sem=rs, device_id=where, device_id_type=MESH
        )

    barrier = pltpu.get_barrier_semaphore()

    def hello(where):
        pl.semaphore_signal(barrier, inc=1, device_id=where, device_id_type=MESH)

    for d in range(1, 16):
        hello(dev(q, (r + d) % 16))
    for d in range(8):
        hello(dev(mate_q, (r + 2 * d) % 16))
    hello(dev(up_q, r))
    hello(dev(down_q, r))

    @pl.when(q != r)
    def _():
        hello(dev(r, q))
        pl.semaphore_wait(barrier, 26)

    @pl.when(q == r)
    def _():
        pl.semaphore_wait(barrier, 25)

    def rows16(ref, at):
        return ref.at[pl.ds(pl.multiple_of(at * 16, 16), 16), :]

    own_q = pl.ds(pl.multiple_of(q * 16, 16), 16)
    sends = []

    trans = rcopy(right_in, rows16(rg, r), t_sem.at[0], t_sem.at[1], dev(r, q))

    @pl.when(q != r)
    def _():
        trans.start()

    @pl.when(q == r)
    def _():
        rg[own_q, :] = right_in[...]

    for d in range(1, 16):
        c = rcopy(left_in, rows16(lg, r), l_send.at[d], l_recv.at[d], dev(q, (r + d) % 16))
        c.start()
        sends.append(c)
    lg[pl.ds(pl.multiple_of(r * 16, 16), 16), :] = left_in[...]

    def right_item(zo, u):
        return rows16(rg, zo * 2 + u)

    def kv_item(zo, u):
        return kvg.at[zo * 2 + u]

    def side(a):
        return x_hi if a == 0 else 1 - x_hi

    def ring_send(item, ss, rs, a, d, k):
        zo = (z + NZ - k) % NZ if d == 0 else (z + k) % NZ
        ref = item(zo, side(a))
        c = rcopy(ref, ref, ss.at[a * 8 + d * 4 + k], rs.at[a * 8 + d * 4 + k], dev(up_q if d == 0 else down_q, r))
        c.start()
        sends.append(c)

    def ring_arrive(item, ss, rs, a, d, k):
        zo = (z + NZ - 1 - k) % NZ if d == 0 else (z + 1 + k) % NZ
        ref = item(zo, side(a))
        rcopy(ref, ref, ss.at[a * 8 + d * 4 + k], rs.at[a * 8 + d * 4 + k], dev(up_q if d == 0 else down_q, r)).wait_recv()
        return zo * 2 + side(a)

    def ring_stage(item, ss, rs, k):
        arrived = []
        for a in range(2):
            for d in range(2):
                if k - 1 < HOPS[a][d]:
                    arrived.append(ring_arrive(item, ss, rs, a, d, k - 1))
                    if k < HOPS[a][d]:
                        ring_send(item, ss, rs, a, d, k)
        return arrived

    right_ring = functools.partial(ring_stage, right_item, r_send, r_recv)
    kv_ring = functools.partial(ring_stage, kv_item, k_send, k_recv)

    kx = rcopy(kv_in.at[1 - x_hi], kvg.at[q], kx_sem.at[0], kx_sem.at[1], dev(mate_q, r))
    kx.start()
    sends.append(kx)
    kvg[q] = kv_in[x_hi]
    for d in range(2):
        ring_send(kv_item, k_send, k_recv, 0, d, 0)

    def fill(e, carry):
        blk = w_ec[pl.ds(pl.multiple_of(e * 32, 32), 32), :]
        none = jnp.zeros_like(blk)
        for i in range(4):
            bd[pl.ds(pl.multiple_of(e * 128 + i * 32, 32), 32), :] = jnp.concatenate(
                [blk if i == n else none for n in range(4)], axis=1
            )
        return carry

    @pl.when(q != r)
    def _():
        rcopy(right_in, rows16(rg, q), t_sem.at[0], t_sem.at[1], dev(r, q)).wait_recv()

    for d in range(2):
        ring_send(right_item, r_send, r_recv, 0, d, 0)
    rx = rcopy(rows16(rg, q), rows16(rg, q), rx_sem.at[0], rx_sem.at[1], dev(mate_q, r))
    rx.start()
    sends.append(rx)
    lax.fori_loop(0, 32, fill, 0)
    rcopy(rows16(rg, q), rows16(rg, mate_q), rx_sem.at[0], rx_sem.at[1], dev(mate_q, r)).wait_recv()
    for d in range(2):
        ring_send(right_item, r_send, r_recv, 1, d, 0)

    rcopy(kv_in.at[0], kvg.at[mate_q], kx_sem.at[0], kx_sem.at[1], dev(mate_q, r)).wait_recv()
    for d in range(2):
        ring_send(kv_item, k_send, k_recv, 1, d, 0)

    def kv_proj(slot):
        at = pl.ds(pl.multiple_of(slot * 64, 64), 64)
        block = kvg[slot, pl.ds(0, 512), :]
        keys = mm(block, wk[...]).astype(BF16)
        values = mm(block, wv[...]).astype(BF16)
        for s in range(8):
            kb[s, at, :] = keys[s * 64 : s * 64 + 64]
            vb[s, at, :] = values[s * 64 : s * 64 + 64]

    right_ring(1)
    kv_proj(q)
    right_ring(2)
    kv_proj(mate_q)
    right_ring(3)
    right_ring(4)
    for d in range(1, 16):
        rcopy(left_in, rows16(lg, (r + 16 - d) % 16), l_send.at[d], l_recv.at[d], dev(q, (r + d) % 16)).wait_recv()
    arrived = kv_ring(1)

    counts = lax.dot_general(rg[:, 2048:2176], lg[:, 2048:2176], (((0,), (0,)), ((), ())), preferred_element_type=F32)
    inv_c[...] = 1.0 / jnp.maximum(counts[0:64], 1.0)
    for n in range(16):
        rt[n * 128 : n * 128 + 128, :] = rg[:, n * 128 : n * 128 + 128].T
    lane = lax.broadcasted_iota(jnp.int32, (64, 128), 1)
    lane8 = lax.broadcasted_iota(jnp.int32, (8, 128), 1)
    own_half = lane8 // 64 == core
    first = core == 0

    def outer_block(t, carry):
        ib = (t + 2 * (1 - core)) % 4
        l_blk = lg[:, pl.ds(pl.multiple_of(ib * 512, 512), 512)]
        for ec in range(4):
            o = mm(rt[ec * 512 : ec * 512 + 512, :], l_blk).astype(BF16)
            for e in range(8):
                for g in range(4):
                    at = (ec * 8 + e) * 128
                    osc[g * 64 : g * 64 + 64, at : at + 128] = o[e * 64 : e * 64 + 64, g * 128 : g * 128 + 128]
        res = mm(osc[...], bd[...])
        for g in range(4):
            norms = []
            for n in range(4):
                i = ib * 16 + g * 4 + n
                scale = jnp.sum(jnp.where(lane == i, inv_c[...], 0.0), axis=1, keepdims=True)
                val = pair_in[i] + res[g * 64 : g * 64 + 64, n * 128 : n * 128 + 128] * scale
                pair_out[i] = val
                cen = val - jnp.mean(val, -1, keepdims=True)
                spread = jnp.mean(cen * cen, -1, keepdims=True)
                norms.append((cen * lax.rsqrt(spread + EPSILON) * pair_gain[...]).astype(BF16))
            b_t = mm(wb_t[...], jnp.concatenate(norms, axis=0), NT)
            tiles = []
            for n in range(2):
                tile = b_t[0:8, n * 128 : n * 128 + 128]
                turned = pltpu.roll(tile, 64, 1)
                tiles.append(jnp.where(own_half, jnp.where(first, tile, turned), 0.0))
                tiles.append(jnp.where(own_half, jnp.where(first, turned, tile), 0.0))
            bias_own[pl.ds(pl.multiple_of(ib * 128 + g * 32, 32), 32), :] = jnp.concatenate(tiles, axis=0).astype(BF16)
        return carry

    half = pl.ds(pl.multiple_of(core * 256, 256), 256)
    far_half = pl.ds(pl.multiple_of((1 - core) * 256, 256), 256)
    lax.fori_loop(0, 2, outer_block, 0)
    sib = rcopy(bias_own.at[far_half, :], bias_sib, b_sem.at[0], b_sem.at[1], dev(q, sib_r))
    sib.start()
    sends.append(sib)
    for slot in arrived:
        kv_proj(slot)
    lax.fori_loop(2, 4, outer_block, 0)
    sib.wait_recv()
    bias_tab[x_hi, kt, half, :] = bias_own[half, :] + bias_sib[...]

    def tab(xx, yy):
        return bias_tab.at[xx // 2, (xx % 2) * 4 + yy, half, :]

    def tab_far(xx, yy):
        return bias_tab.at[xx // 2, (xx % 2) * 4 + yy, far_half, :]

    for d in range(1, 16):
        xx, yy = (x + d // 4) % 4, (y + d % 4) % 4
        where = dev(z * 2 + xx // 2, (xx % 2) * 8 + yy * 2 + core)
        c = rcopy(tab(x, y), tab(x, y), pl_send.at[d], pl_recv.at[d], where)
        c.start()
        sends.append(c)
    c = rcopy(tab(x, y), tab(x, y), f_send.at[0], f_recv.at[0], dev(q, sib_r))
    c.start()
    sends.append(c)
    arrived = kv_ring(2)
    for slot in arrived:
        kv_proj(slot)
    for d in range(1, 16):
        xx, yy = (x + 4 - d // 4) % 4, (y + 4 - d % 4) % 4
        got = tab(xx, yy)
        rcopy(got, got, pl_send.at[d], pl_recv.at[d], dev(q, sib_r)).wait_recv()
        c = rcopy(got, got, f_send.at[d], f_recv.at[d], dev(q, sib_r))
        c.start()
        sends.append(c)
    arrived = kv_ring(3)
    for slot in arrived:
        kv_proj(slot)
    for d in range(16):
        xx, yy = (x + 4 - d // 4) % 4, (y + 4 - d % 4) % 4
        got = tab_far(xx, yy)
        rcopy(got, got, f_send.at[d], f_recv.at[d], dev(q, sib_r)).wait_recv()
    arrived = kv_ring(4)
    for slot in arrived:
        kv_proj(slot)

    for n in range(8):
        live = kvg[2 * n, pl.ds(512, 16), 0:128].astype(F32) + kvg[2 * n + 1, pl.ds(512, 16), 0:128].astype(F32)
        mask_tab[:, n * 128 : n * 128 + 128] = jnp.where(live > 0.5, 0.0, MASKED)

    lane_head = lax.broadcasted_iota(jnp.int32, (64, 128), 1) // 32

    def by_head(ref, tile):
        out = ref[pl.ds(tile * 4, 64, stride=8), :]
        for h in range(1, 4):
            out = jnp.where(lane_head == h, ref[pl.ds(tile * 4 + h, 64, stride=8), :], out)
        return out

    def attend(v, dest):
        def one(s, carry):
            at = pl.ds(pl.multiple_of(s * 64, 64), 64)
            block = kvg[z * 2 + v, at, :]
            queries = (mm(block, wq[...]) * 32**-0.5).astype(BF16)
            gates = jax.nn.sigmoid(mm(block, wg[...]))
            spread_q = (mm(expand[...], queries) * head_mask[...]).astype(BF16)
            sc_buf[...] = mm(spread_q, kb[s], NT)
            m_row = mask_tab[pl.ds(s, 1), :]
            for rb in range(16):
                rows = pl.ds(rb * 32, 32)
                bias = jnp.concatenate([bias_tab[v, n, rows, :].astype(F32) for n in range(8)], axis=1)
                sc = sc_buf[rows, :] + bias + m_row
                w = jnp.exp(sc - jnp.max(sc, -1, keepdims=True))
                tot_buf[rows, :] = jnp.broadcast_to(jnp.sum(w, -1, keepdims=True), (32, 128))
                p_buf[rows, :] = w.astype(BF16)
            mixed = mm(p_buf[...], vb[s])
            for tile in range(2):
                r_buf[tile] = mixed[:, tile * 128 : tile * 128 + 128]
                num = by_head(r_buf.at[tile], tile)
                den = by_head(tot_buf, tile)
                dest[at, pl.ds(tile * 128, 128)] = (num / den * gates[:, tile * 128 : tile * 128 + 128]).astype(BF16)
            return carry

        lax.fori_loop(0, 8, one, 0)

    def finish(gated, which):
        def part(n, carry):
            at = pl.ds(pl.multiple_of(n * 256, 256), 256)
            after = align_in[which, at, :].astype(F32) + mm(gated[at, :], wo[...])
            cen = after - jnp.mean(after, -1, keepdims=True)
            spread = jnp.mean(cen * cen, -1, keepdims=True)
            norm = (cen * lax.rsqrt(spread + EPSILON) * t_gain[...]).astype(BF16)
            hidden = jnp.maximum(mm(norm, w_up[...]), 0.0).astype(BF16)
            align_out[which, at, :] = after + mm(hidden, w_down[...])
            return carry

        lax.fori_loop(0, 2, part, 0)

    attend(1 - x_hi, gate_far)
    back = rcopy(gate_far, gate_in, g_sem.at[0], g_sem.at[1], dev(mate_q, r))
    back.start()
    sends.append(back)
    attend(x_hi, gate_own)
    finish(gate_own, x_hi)
    back.wait_recv()
    finish(gate_in, 1 - x_hi)

    @pl.when(q != r)
    def _():
        trans.wait_send()

    for c in sends:
        c.wait_send()


def on_device(
    alignment, alignment_mask, residue_mask, pair_input, outer_gain, left_weight, right_weight, outer_weight, pair_gain,
    bias_weight, row_gain, query_weight, key_weight, value_weight, gate_weight, output_weight, transition_gain, up_weight,
    down_weight,
):
    q = lax.axis_index("seq")
    x_hi = q % 2
    live = alignment_mask * lax.dynamic_slice_in_dim(residue_mask, q * 64, 64)[None, :]
    live_f = live.astype(F32)
    live_b = live.astype(BF16)
    values = alignment.astype(F32)
    center = values - jnp.mean(values, -1, keepdims=True)
    spread = jnp.mean(center * center, -1, keepdims=True)
    norm = center * lax.rsqrt(spread + EPSILON)
    outer_norm = (norm * outer_gain).astype(BF16)
    row_norm = (norm * row_gain).astype(BF16)
    both = jnp.dot(
        outer_norm.reshape(1024, 256),
        jnp.concatenate([left_weight, right_weight], axis=1),
        preferred_element_type=F32,
    ).reshape(16, 64, 64)
    both = (both * live_f[..., None]).astype(BF16)
    flags = jnp.pad(live_b, ((0, 0), (0, 64)))
    left = jnp.concatenate([both[..., :32].reshape(16, 2048), flags], axis=1)
    right = jnp.concatenate([both[..., 32:].transpose(0, 2, 1).reshape(16, 2048), flags], axis=1)
    none = jnp.zeros_like(live_b)
    marks = jnp.where(x_hi == 0, jnp.concatenate([live_b, none], axis=1), jnp.concatenate([none, live_b], axis=1))
    marks = jnp.pad(marks.reshape(2, 8, 128), ((0, 0), (0, 8), (0, 128)))
    kv = jnp.concatenate([row_norm.reshape(2, 512, 256), marks], axis=1)
    w_ec = outer_weight.reshape(32, 32, 128).transpose(1, 0, 2).reshape(1024, 128)
    wb_t = jnp.pad(bias_weight.T, ((0, 8), (0, 0)))
    at = jnp.arange(512)
    expand = (at[:, None] // 8 == jnp.arange(64)[None, :]).astype(BF16)
    head_mask = (at[:, None] % 8 == jnp.arange(256)[None, :] // 32).astype(F32)

    vm = pl.BlockSpec(memory_space=pltpu.VMEM)
    dma, v = pltpu.SemaphoreType.DMA, pltpu.VMEM
    pair_out, align_out = pl.pallas_call(
        kernel,
        out_shape=(jax.ShapeDtypeStruct((64, 64, 128), F32), jax.ShapeDtypeStruct((2, 512, 256), F32)),
        in_specs=[vm] * 18,
        out_specs=(vm, vm),
        scratch_shapes=[
            v((256, 2176), BF16), v((256, 2176), BF16), v((2048, 256), BF16), v((4096, 512), BF16), v((256, 4096), BF16),
            v((64, 128), F32), v((512, 128), BF16), v((256, 128), BF16), v((2, 8, 512, 128), BF16),
            v((16, 528, 256), BF16), v((8, 1024, 256), BF16), v((8, 1024, 256), BF16), v((16, 1024), F32),
            v((512, 1024), F32), v((512, 1024), BF16), v((2, 512, 128), F32), v((512, 128), F32),
            v((512, 256), BF16), v((512, 256), BF16), v((512, 256), BF16),
            dma((16,)), dma((16,)), dma((2,)), dma((2,)), dma((2,)), dma((16,)), dma((16,)), dma((16,)), dma((16,)),
            dma((2,)), dma((16,)), dma((16,)), dma((16,)), dma((16,)), dma((2,)),
        ],
        compiler_params=pltpu.CompilerParams(collective_id=0, has_side_effects=True, vmem_limit_bytes=60 << 20),
    )(
        left, right, kv, pair_input, alignment.reshape(2, 512, 256), w_ec, wb_t, pair_gain.reshape(1, 128), query_weight,
        gate_weight, key_weight, value_weight, output_weight, transition_gain.reshape(1, 256), up_weight, down_weight,
        expand, head_mask,
    )
    return pair_out, align_out.reshape(16, 64, 256)


def solution(mesh):
    rep = P()
    in_specs = (P("res", "seq", None), P("res", "seq"), rep, P("seq", "res", None)) + (rep,) * 15
    out_specs = (P("seq", "res", None), P("res", "seq", None))
    return jax.shard_map(on_device, mesh=mesh, in_specs=in_specs, out_specs=out_specs, check_vma=False)
```

```python
import functools

import jax
import jax.numpy as jnp
from jax import lax
from jax.experimental import pallas as pl
from jax.experimental.pallas import tpu as pltpu
from jax.sharding import PartitionSpec as P

EPSILON = 1e-05
MASKED = -1000000000.0
MESH = pl.DeviceIdType.MESH
F32, BF16 = jnp.float32, jnp.bfloat16
NN = (((1,), (0,)), ((), ()))
NT = (((1,), (1,)), ((), ()))
NZ = 8
HOPS = ((4, 3), (3, 4))


def mm(a, b, dims=NN):
    return lax.dot_general(a, b, dims, preferred_element_type=F32)


def kernel(
    align_in, a_mask, r_mask, o_gain, wl_t, wr_t, p_gain, wb_t, row_gain, t_gain,
    pair_hbm, ow_hbm, wq_hbm, wk_hbm, wv_hbm, wg_hbm, wo_hbm, up_hbm, down_hbm,
    pair_hbm_out, align_out,
    left_in, right_in, kv_in, on, live_f, turn, pair_in, pair_out, w_bf, w_f32, wq, wk, wv, wg, wo, w_up, w_down,
    expand, head_mask, in_sem,
    lg, rg, rt, bd, osc, inv_c, bias_own, bias_sib, bias_tab, kvg, kb, vb, mask_tab, sc_buf, p_buf, r_buf, tot_buf,
    gate_own, gate_far, gate_in,
    l_send, l_recv, t_sem, rx_sem, kx_sem, r_send, r_recv, k_send, k_recv, b_sem, pl_send, pl_recv, f_send, f_recv, g_sem,
):
    q = lax.axis_index("seq")
    r = lax.axis_index("res")
    z, x_hi = q // 2, q % 2
    core = r % 2
    y = (r // 2) % 4
    x_lo = r // 8
    x = x_hi * 2 + x_lo
    kt = r // 2
    mate_q = q + 1 - 2 * x_hi
    sib_r = r + 1 - 2 * core
    up_q = ((z + 1) % NZ) * 2 + x_hi
    down_q = ((z + NZ - 1) % NZ) * 2 + x_hi

    def dev(qq, rr):
        return {"seq": qq, "res": rr}

    def rcopy(src, dst, ss, rs, where):
        return pltpu.make_async_remote_copy(
            src_ref=src, dst_ref=dst, send_sem=ss, recv_sem=rs, device_id=where, device_id_type=MESH
        )

    barrier = pltpu.get_barrier_semaphore()

    def hello(where):
        pl.semaphore_signal(barrier, inc=1, device_id=where, device_id_type=MESH)

    for d in range(1, 16):
        hello(dev(q, (r + d) % 16))
    for d in range(8):
        hello(dev(mate_q, (r + 2 * d) % 16))
    hello(dev(up_q, r))
    hello(dev(down_q, r))

    @pl.when(q != r)
    def _():
        hello(dev(r, q))

    loads = [
        pltpu.make_async_copy(src, dst, in_sem.at[n])
        for n, (src, dst) in enumerate(
            (
                (ow_hbm, w_bf), (wk_hbm, wk), (wv_hbm, wv), (pair_hbm, pair_in), (wq_hbm, wq), (wg_hbm, wg), (wo_hbm, wo),
                (up_hbm, w_up), (down_hbm, w_down),
            )
        )
    ]
    for c in loads:
        c.start()

    def iota(shape, dim):
        return lax.broadcasted_iota(jnp.int32, shape, dim)

    flag_row = r_mask[pl.ds(q // 2, 1), :].astype(F32)
    flag_row = jnp.where(x_hi == 0, flag_row, pltpu.roll(flag_row, 64, 1))
    live_f[...] = jnp.zeros_like(live_f)
    live_f[:, 0:64] = a_mask[...].astype(F32) * flag_row[:, 0:64]
    live = live_f[...]
    live_b = live.astype(BF16)

    def norms(n, carry):
        at = pl.ds(pl.multiple_of(n * 256, 256), 256)
        vals = align_in[n // 2, pl.ds(pl.multiple_of((n % 2) * 256, 256), 256), :].astype(F32)
        cen = vals - jnp.mean(vals, -1, keepdims=True)
        spread = jnp.mean(cen * cen, -1, keepdims=True)
        norm = cen * lax.rsqrt(spread + EPSILON)
        pick = (iota((256, 16), 0) // 64 + n * 4 == iota((256, 16), 1)).astype(F32).astype(BF16)
        flags = mm(pick, live_b)
        flag = jnp.sum(jnp.where(iota((256, 128), 0) % 64 == iota((256, 128), 1), flags, 0.0), -1, keepdims=True)
        on[at, :] = (norm * o_gain[...] * flag).astype(BF16)
        kv_in[n // 2, pl.ds(pl.multiple_of((n % 2) * 256, 256), 256), :] = (norm * row_gain[...]).astype(BF16)
        return carry

    lax.fori_loop(0, 4, norms, 0)
    marks = jnp.where(x_hi == 0, live, pltpu.roll(live, 64, 1))
    for h in range(2):
        kv_in[h, pl.ds(512, 16), 0:128] = jnp.concatenate(
            [marks[h * 8 : h * 8 + 8], jnp.zeros((8, 128), F32)], axis=0
        ).astype(BF16)
        kv_in[h, pl.ds(512, 16), 128:256] = jnp.zeros((16, 128), BF16)
    r_t = mm(wr_t[...], on[...], NT)
    for n in range(8):
        tile = r_t[:, n * 128 : n * 128 + 128]
        turn[n * 64 : n * 64 + 32, :] = tile
        turn[n * 64 + 32 : n * 64 + 64, :] = pltpu.roll(tile, 64, 1)
    low = iota((16, 128), 1) < 64
    for n in range(16):
        even = turn[pl.ds(2 * n, 16, stride=32), :]
        odd = turn[pl.ds(2 * n + 1, 16, stride=32), :]
        right_in[:, n * 128 : n * 128 + 128] = jnp.where(low, even, pltpu.roll(odd, 64, 1)).astype(BF16)
    right_in[:, 2048:2176] = live_b
    four = jnp.concatenate([wl_t[...]] * 4, axis=0)
    l_all = mm(on[...], four, NT)
    l_all = jnp.where(iota((1024, 128), 0) % 4 == iota((1024, 128), 1) // 32, l_all, 0.0).astype(BF16)
    to, fro = iota((256, 1024), 0), iota((256, 1024), 1)
    pick = ((fro // 64 == to % 16) & ((fro % 64) // 4 == to // 16)).astype(F32).astype(BF16)
    l_rows = mm(pick, l_all).astype(BF16)
    for n in range(16):
        left_in[:, n * 128 : n * 128 + 128] = l_rows[n * 16 : n * 16 + 16]
    left_in[:, 2048:2176] = live_b

    @pl.when(q != r)
    def _():
        pl.semaphore_wait(barrier, 26)

    @pl.when(q == r)
    def _():
        pl.semaphore_wait(barrier, 25)

    def rows16(ref, at):
        return ref.at[pl.ds(pl.multiple_of(at * 16, 16), 16), :]

    own_q = pl.ds(pl.multiple_of(q * 16, 16), 16)
    sends = []

    trans = rcopy(right_in, rows16(rg, r), t_sem.at[0], t_sem.at[1], dev(r, q))

    @pl.when(q != r)
    def _():
        trans.start()

    @pl.when(q == r)
    def _():
        rg[own_q, :] = right_in[...]

    for d in range(1, 16):
        c = rcopy(left_in, rows16(lg, r), l_send.at[d], l_recv.at[d], dev(q, (r + d) % 16))
        c.start()
        sends.append(c)
    lg[pl.ds(pl.multiple_of(r * 16, 16), 16), :] = left_in[...]

    def right_item(zo, u):
        return rows16(rg, zo * 2 + u)

    def kv_item(zo, u):
        return kvg.at[zo * 2 + u]

    def side(a):
        return x_hi if a == 0 else 1 - x_hi

    def ring_send(item, ss, rs, a, d, k):
        zo = (z + NZ - k) % NZ if d == 0 else (z + k) % NZ
        ref = item(zo, side(a))
        c = rcopy(ref, ref, ss.at[a * 8 + d * 4 + k], rs.at[a * 8 + d * 4 + k], dev(up_q if d == 0 else down_q, r))
        c.start()
        sends.append(c)

    def ring_arrive(item, ss, rs, a, d, k):
        zo = (z + NZ - 1 - k) % NZ if d == 0 else (z + 1 + k) % NZ
        ref = item(zo, side(a))
        rcopy(ref, ref, ss.at[a * 8 + d * 4 + k], rs.at[a * 8 + d * 4 + k], dev(up_q if d == 0 else down_q, r)).wait_recv()
        return zo * 2 + side(a)

    def ring_stage(item, ss, rs, k):
        arrived = []
        for a in range(2):
            for d in range(2):
                if k - 1 < HOPS[a][d]:
                    arrived.append(ring_arrive(item, ss, rs, a, d, k - 1))
                    if k < HOPS[a][d]:
                        ring_send(item, ss, rs, a, d, k)
        return arrived

    right_ring = functools.partial(ring_stage, right_item, r_send, r_recv)
    kv_ring = functools.partial(ring_stage, kv_item, k_send, k_recv)

    kx = rcopy(kv_in.at[1 - x_hi], kvg.at[q], kx_sem.at[0], kx_sem.at[1], dev(mate_q, r))
    kx.start()
    sends.append(kx)
    kvg[q] = kv_in[x_hi]
    for d in range(2):
        ring_send(kv_item, k_send, k_recv, 0, d, 0)

    def fill(e, carry):
        blk = w_f32[pl.ds(e, 32, stride=32), :].astype(BF16)
        none = jnp.zeros_like(blk)
        for i in range(4):
            bd[pl.ds(pl.multiple_of(e * 128 + i * 32, 32), 32), :] = jnp.concatenate(
                [blk if i == n else none for n in range(4)], axis=1
            )
        return carry

    @pl.when(q != r)
    def _():
        rcopy(right_in, rows16(rg, q), t_sem.at[0], t_sem.at[1], dev(r, q)).wait_recv()

    for d in range(2):
        ring_send(right_item, r_send, r_recv, 0, d, 0)
    rx = rcopy(rows16(rg, q), rows16(rg, q), rx_sem.at[0], rx_sem.at[1], dev(mate_q, r))
    rx.start()
    sends.append(rx)
    loads[0].wait()
    w_f32[...] = w_bf[...].astype(F32)
    lax.fori_loop(0, 32, fill, 0)
    expand[...] = (iota((512, 64), 0) // 8 == iota((512, 64), 1)).astype(F32).astype(BF16)
    head_mask[...] = (iota((512, 256), 0) % 8 == iota((512, 256), 1) // 32).astype(F32)
    loads[1].wait()
    loads[2].wait()
    rcopy(rows16(rg, q), rows16(rg, mate_q), rx_sem.at[0], rx_sem.at[1], dev(mate_q, r)).wait_recv()
    for d in range(2):
        ring_send(right_item, r_send, r_recv, 1, d, 0)

    rcopy(kv_in.at[0], kvg.at[mate_q], kx_sem.at[0], kx_sem.at[1], dev(mate_q, r)).wait_recv()
    for d in range(2):
        ring_send(kv_item, k_send, k_recv, 1, d, 0)

    def kv_proj(slot):
        at = pl.ds(pl.multiple_of(slot * 64, 64), 64)
        block = kvg[slot, pl.ds(0, 512), :]
        keys = mm(block, wk[...]).astype(BF16)
        values = mm(block, wv[...]).astype(BF16)
        for s in range(8):
            kb[s, at, :] = keys[s * 64 : s * 64 + 64]
            vb[s, at, :] = values[s * 64 : s * 64 + 64]

    right_ring(1)
    kv_proj(q)
    right_ring(2)
    kv_proj(mate_q)
    right_ring(3)
    right_ring(4)
    for d in range(1, 16):
        rcopy(left_in, rows16(lg, (r + 16 - d) % 16), l_send.at[d], l_recv.at[d], dev(q, (r + d) % 16)).wait_recv()
    arrived = kv_ring(1)

    loads[3].wait()

    counts = lax.dot_general(rg[:, 2048:2176], lg[:, 2048:2176], (((0,), (0,)), ((), ())), preferred_element_type=F32)
    inv_c[...] = 1.0 / jnp.maximum(counts[0:64], 1.0)
    for n in range(16):
        rt[n * 128 : n * 128 + 128, :] = rg[:, n * 128 : n * 128 + 128].T
    lane = lax.broadcasted_iota(jnp.int32, (64, 128), 1)
    lane8 = lax.broadcasted_iota(jnp.int32, (8, 128), 1)
    own_half = lane8 // 64 == core
    first = core == 0

    def outer_block(t, carry):
        ib = (t + 2 * (1 - core)) % 4
        l_blk = lg[:, pl.ds(pl.multiple_of(ib * 512, 512), 512)]
        for ec in range(4):
            o = mm(rt[ec * 512 : ec * 512 + 512, :], l_blk).astype(BF16)
            for e in range(8):
                for g in range(4):
                    at = (ec * 8 + e) * 128
                    osc[g * 64 : g * 64 + 64, at : at + 128] = o[e * 64 : e * 64 + 64, g * 128 : g * 128 + 128]
        res = mm(osc[...], bd[...])
        for g in range(4):
            norms = []
            for n in range(4):
                i = ib * 16 + g * 4 + n
                scale = jnp.sum(jnp.where(lane == i, inv_c[...], 0.0), axis=1, keepdims=True)
                val = pair_in[i] + res[g * 64 : g * 64 + 64, n * 128 : n * 128 + 128] * scale
                pair_out[i] = val
                cen = val - jnp.mean(val, -1, keepdims=True)
                spread = jnp.mean(cen * cen, -1, keepdims=True)
                norms.append((cen * lax.rsqrt(spread + EPSILON) * p_gain[...]).astype(BF16))
            b_t = mm(wb_t[...], jnp.concatenate(norms, axis=0), NT)
            tiles = []
            for n in range(2):
                tile = b_t[0:8, n * 128 : n * 128 + 128]
                turned = pltpu.roll(tile, 64, 1)
                tiles.append(jnp.where(own_half, jnp.where(first, tile, turned), 0.0))
                tiles.append(jnp.where(own_half, jnp.where(first, turned, tile), 0.0))
            bias_own[pl.ds(pl.multiple_of(ib * 128 + g * 32, 32), 32), :] = jnp.concatenate(tiles, axis=0).astype(BF16)
        return carry

    half = pl.ds(pl.multiple_of(core * 256, 256), 256)
    far_half = pl.ds(pl.multiple_of((1 - core) * 256, 256), 256)
    lax.fori_loop(0, 2, outer_block, 0)
    sib = rcopy(bias_own.at[far_half, :], bias_sib, b_sem.at[0], b_sem.at[1], dev(q, sib_r))
    sib.start()
    sends.append(sib)
    for slot in arrived:
        kv_proj(slot)
    lax.fori_loop(2, 4, outer_block, 0)
    pair_back = pltpu.make_async_copy(pair_out, pair_hbm_out, in_sem.at[9])
    pair_back.start()
    sib.wait_recv()
    bias_tab[x_hi, kt, half, :] = bias_own[half, :] + bias_sib[...]

    def tab(xx, yy):
        return bias_tab.at[xx // 2, (xx % 2) * 4 + yy, half, :]

    def tab_far(xx, yy):
        return bias_tab.at[xx // 2, (xx % 2) * 4 + yy, far_half, :]

    for d in range(1, 16):
        xx, yy = (x + d // 4) % 4, (y + d % 4) % 4
        where = dev(z * 2 + xx // 2, (xx % 2) * 8 + yy * 2 + core)
        c = rcopy(tab(x, y), tab(x, y), pl_send.at[d], pl_recv.at[d], where)
        c.start()
        sends.append(c)
    c = rcopy(tab(x, y), tab(x, y), f_send.at[0], f_recv.at[0], dev(q, sib_r))
    c.start()
    sends.append(c)
    arrived = kv_ring(2)
    for slot in arrived:
        kv_proj(slot)
    for d in range(1, 16):
        xx, yy = (x + 4 - d // 4) % 4, (y + 4 - d % 4) % 4
        got = tab(xx, yy)
        rcopy(got, got, pl_send.at[d], pl_recv.at[d], dev(q, sib_r)).wait_recv()
        c = rcopy(got, got, f_send.at[d], f_recv.at[d], dev(q, sib_r))
        c.start()
        sends.append(c)
    arrived = kv_ring(3)
    for slot in arrived:
        kv_proj(slot)
    for d in range(16):
        xx, yy = (x + 4 - d // 4) % 4, (y + 4 - d % 4) % 4
        got = tab_far(xx, yy)
        rcopy(got, got, f_send.at[d], f_recv.at[d], dev(q, sib_r)).wait_recv()
    arrived = kv_ring(4)
    for slot in arrived:
        kv_proj(slot)

    for n in range(8):
        live = kvg[2 * n, pl.ds(512, 16), 0:128].astype(F32) + kvg[2 * n + 1, pl.ds(512, 16), 0:128].astype(F32)
        mask_tab[:, n * 128 : n * 128 + 128] = jnp.where(live > 0.5, 0.0, MASKED)

    lane_head = lax.broadcasted_iota(jnp.int32, (64, 128), 1) // 32

    def by_head(ref, tile):
        out = ref[pl.ds(tile * 4, 64, stride=8), :]
        for h in range(1, 4):
            out = jnp.where(lane_head == h, ref[pl.ds(tile * 4 + h, 64, stride=8), :], out)
        return out

    for c in loads[4:]:
        c.wait()

    def attend(v, dest):
        def rows_of(s):
            return pl.ds(pl.multiple_of(s * 64, 64), 64)

        def look(s, slot):
            queries = (mm(kvg[z * 2 + v, rows_of(s), :], wq[...]) * 32**-0.5).astype(BF16)
            spread_q = (mm(expand[...], queries) * head_mask[...]).astype(BF16)
            sc_buf[slot] = mm(spread_q, kb[s], NT)

        def weigh(s, slot):
            m_row = mask_tab[pl.ds(s, 1), :]
            for rb in range(16):
                rows = pl.ds(rb * 32, 32)
                bias = jnp.concatenate([bias_tab[v, n, rows, :].astype(F32) for n in range(8)], axis=1)
                sc = sc_buf[slot, rows, :] + bias + m_row
                w = jnp.exp(sc - jnp.max(sc, -1, keepdims=True))
                tot_buf[slot, rows, :] = jnp.broadcast_to(jnp.sum(w, -1, keepdims=True), (32, 128))
                p_buf[slot, rows, :] = w.astype(BF16)

        def mix(s, slot):
            gates = jax.nn.sigmoid(mm(kvg[z * 2 + v, rows_of(s), :], wg[...]))
            mixed = mm(p_buf[slot], vb[s])
            for tile in range(2):
                r_buf[slot, tile] = mixed[:, tile * 128 : tile * 128 + 128]
                num = by_head(r_buf.at[slot, tile], tile)
                den = by_head(tot_buf.at[slot], tile)
                dest[rows_of(s), pl.ds(tile * 128, 128)] = (
                    num / den * gates[:, tile * 128 : tile * 128 + 128]
                ).astype(BF16)

        def two(n, carry):
            s = n * 2
            look(s + 1, 1)
            weigh(s, 0)
            mix(s, 0)
            weigh(s + 1, 1)
            look(lax.rem(s + 2, 8), 0)
            mix(s + 1, 1)
            return carry

        look(0, 0)
        lax.fori_loop(0, 4, two, 0)

    def finish(gated, which):
        def part(n, carry):
            at = pl.ds(pl.multiple_of(n * 256, 256), 256)
            after = align_in[which, at, :].astype(F32) + mm(gated[at, :], wo[...])
            cen = after - jnp.mean(after, -1, keepdims=True)
            spread = jnp.mean(cen * cen, -1, keepdims=True)
            norm = (cen * lax.rsqrt(spread + EPSILON) * t_gain[...]).astype(BF16)
            hidden = jnp.maximum(mm(norm, w_up[...]), 0.0).astype(BF16)
            align_out[which, at, :] = after + mm(hidden, w_down[...])
            return carry

        lax.fori_loop(0, 2, part, 0)

    attend(1 - x_hi, gate_far)
    back = rcopy(gate_far, gate_in, g_sem.at[0], g_sem.at[1], dev(mate_q, r))
    back.start()
    sends.append(back)
    attend(x_hi, gate_own)
    finish(gate_own, x_hi)
    back.wait_recv()
    finish(gate_in, 1 - x_hi)

    @pl.when(q != r)
    def _():
        trans.wait_send()

    for c in sends:
        c.wait_send()
    pair_back.wait()


def on_device(
    alignment, alignment_mask, residue_mask, pair_input, outer_gain, left_weight, right_weight, outer_weight, pair_gain,
    bias_weight, row_gain, query_weight, key_weight, value_weight, gate_weight, output_weight, transition_gain, up_weight,
    down_weight,
):
    vm = pl.BlockSpec(memory_space=pltpu.VMEM)
    hbm = pl.BlockSpec(memory_space=pl.ANY)
    dma, v = pltpu.SemaphoreType.DMA, pltpu.VMEM
    pair_out, align_out = pl.pallas_call(
        kernel,
        out_shape=(jax.ShapeDtypeStruct((64, 64, 128), F32), jax.ShapeDtypeStruct((2, 512, 256), F32)),
        in_specs=[vm] * 10 + [hbm] * 9,
        out_specs=(hbm, vm),
        scratch_shapes=[
            v((16, 2176), BF16), v((16, 2176), BF16), v((2, 528, 256), BF16), v((1024, 256), BF16), v((16, 128), F32),
            v((512, 128), F32), v((64, 64, 128), F32), v((64, 64, 128), F32), v((1024, 128), BF16), v((1024, 128), F32),
            v((256, 256), BF16), v((256, 256), BF16), v((256, 256), BF16), v((256, 256), BF16), v((256, 256), BF16),
            v((256, 1024), BF16), v((1024, 256), BF16), v((512, 64), BF16), v((512, 256), F32), dma((10,)),
            v((256, 2176), BF16), v((256, 2176), BF16), v((2048, 256), BF16), v((4096, 512), BF16), v((256, 4096), BF16),
            v((64, 128), F32), v((512, 128), BF16), v((256, 128), BF16), v((2, 8, 512, 128), BF16),
            v((16, 528, 256), BF16), v((8, 1024, 256), BF16), v((8, 1024, 256), BF16), v((16, 1024), F32),
            v((2, 512, 1024), F32), v((2, 512, 1024), BF16), v((2, 2, 512, 128), F32), v((2, 512, 128), F32),
            v((512, 256), BF16), v((512, 256), BF16), v((512, 256), BF16),
            dma((16,)), dma((16,)), dma((2,)), dma((2,)), dma((2,)), dma((16,)), dma((16,)), dma((16,)), dma((16,)),
            dma((2,)), dma((16,)), dma((16,)), dma((16,)), dma((16,)), dma((2,)),
        ],
        compiler_params=pltpu.CompilerParams(collective_id=0, has_side_effects=True, vmem_limit_bytes=60 << 20),
    )(
        alignment.reshape(2, 512, 256), alignment_mask, residue_mask.reshape(8, 128), outer_gain.reshape(1, 256), left_weight.T,
        right_weight.T, pair_gain.reshape(1, 128), bias_weight.T, row_gain.reshape(1, 256), transition_gain.reshape(1, 256),
        pair_input, outer_weight, query_weight, key_weight, value_weight, gate_weight, output_weight, up_weight, down_weight,
    )
    return pair_out, align_out.reshape(16, 64, 256)


def solution(mesh):
    rep = P()
    in_specs = (P("res", "seq", None), P("res", "seq"), rep, P("seq", "res", None)) + (rep,) * 15
    out_specs = (P("seq", "res", None), P("res", "seq", None))
    return jax.shard_map(on_device, mesh=mesh, in_specs=in_specs, out_specs=out_specs, check_vma=False)
```

```python
import functools

import jax
import jax.numpy as jnp
from jax import lax
from jax.experimental import pallas as pl
from jax.experimental.pallas import tpu as pltpu
from jax.sharding import PartitionSpec as P

EPSILON = 1e-05
MASKED = -1000000000.0
MESH = pl.DeviceIdType.MESH
F32, BF16 = jnp.float32, jnp.bfloat16
NN = (((1,), (0,)), ((), ()))
NT = (((1,), (1,)), ((), ()))
NZ = 8
HOPS = ((4, 3), (3, 4))


def mm(a, b, dims=NN):
    return lax.dot_general(a, b, dims, preferred_element_type=F32)


def kernel(
    align_in, a_mask, r_mask, o_gain, wl_t, wr_t, p_gain, wb_t, row_gain, t_gain,
    pair_hbm, ow_hbm, wq_hbm, wk_hbm, wv_hbm, wg_hbm, wo_hbm, up_hbm, down_hbm,
    pair_hbm_out, align_out,
    left_in, right_in, kv_in, on, live_f, turn, pair_in, pair_out, w_bf, w_f32, wq, wk, wv, wg, wo, w_up, w_down,
    expand, head_mask, in_sem,
    lg, rg, rt, bd, osc, inv_c, bias_own, bias_sib, bias_tab, kvg, kb, vb, mask_tab, sc_buf, p_buf, r_buf, tot_buf,
    gate_own, gate_far, gate_in,
    l_send, l_recv, t_sem, rx_send, rx_recv, kx_sem, r_send, r_recv, k_send, k_recv, b_sem, pl_send, pl_recv, f_send, f_recv,
    g_sem,
):
    q = lax.axis_index("seq")
    r = lax.axis_index("res")
    z, x_hi = q // 2, q % 2
    core = r % 2
    y = (r // 2) % 4
    x_lo = r // 8
    x = x_hi * 2 + x_lo
    kt = r // 2
    mate_q = q + 1 - 2 * x_hi
    sib_r = r + 1 - 2 * core
    up_q = ((z + 1) % NZ) * 2 + x_hi
    down_q = ((z + NZ - 1) % NZ) * 2 + x_hi

    def dev(qq, rr):
        return {"seq": qq, "res": rr}

    def rcopy(src, dst, ss, rs, where):
        return pltpu.make_async_remote_copy(
            src_ref=src, dst_ref=dst, send_sem=ss, recv_sem=rs, device_id=where, device_id_type=MESH
        )

    barrier = pltpu.get_barrier_semaphore()

    def hello(where):
        pl.semaphore_signal(barrier, inc=1, device_id=where, device_id_type=MESH)

    for d in range(1, 8):
        hello(dev(q, (r + 2 * d) % 16))
    hello(dev(q, sib_r))
    for d in range(8):
        hello(dev(mate_q, (r + 2 * d) % 16))
    hello(dev(up_q, r))
    hello(dev(down_q, r))

    @pl.when(q != r)
    def _():
        hello(dev(r, q))

    loads = [
        pltpu.make_async_copy(src, dst, in_sem.at[n])
        for n, (src, dst) in enumerate(
            (
                (ow_hbm, w_bf), (wk_hbm, wk), (wv_hbm, wv), (pair_hbm, pair_in), (wq_hbm, wq), (wg_hbm, wg), (wo_hbm, wo),
                (up_hbm, w_up), (down_hbm, w_down),
            )
        )
    ]
    for c in loads:
        c.start()

    def iota(shape, dim):
        return lax.broadcasted_iota(jnp.int32, shape, dim)

    flag_row = r_mask[pl.ds(q // 2, 1), :].astype(F32)
    flag_row = jnp.where(x_hi == 0, flag_row, pltpu.roll(flag_row, 64, 1))
    live_f[...] = jnp.zeros_like(live_f)
    live_f[:, 0:64] = a_mask[...].astype(F32) * flag_row[:, 0:64]
    live = live_f[...]
    live_b = live.astype(BF16)

    def norms(n, carry):
        at = pl.ds(pl.multiple_of(n * 256, 256), 256)
        vals = align_in[n // 2, pl.ds(pl.multiple_of((n % 2) * 256, 256), 256), :].astype(F32)
        cen = vals - jnp.mean(vals, -1, keepdims=True)
        spread = jnp.mean(cen * cen, -1, keepdims=True)
        norm = cen * lax.rsqrt(spread + EPSILON)
        pick = (iota((256, 16), 0) // 64 + n * 4 == iota((256, 16), 1)).astype(F32).astype(BF16)
        flags = mm(pick, live_b)
        flag = jnp.sum(jnp.where(iota((256, 128), 0) % 64 == iota((256, 128), 1), flags, 0.0), -1, keepdims=True)
        on[at, :] = (norm * o_gain[...] * flag).astype(BF16)
        kv_in[n // 2, pl.ds(pl.multiple_of((n % 2) * 272, 16), 256), :] = (norm * row_gain[...]).astype(BF16)
        return carry

    lax.fori_loop(0, 4, norms, 0)
    marks = jnp.where(x_hi == 0, live, pltpu.roll(live, 64, 1))
    for h in range(2):
        for g in range(2):
            kv_in[h, pl.ds(g * 272 + 256, 16), 0:128] = jnp.concatenate(
                [marks[h * 8 : h * 8 + 8], jnp.zeros((8, 128), F32)], axis=0
            ).astype(BF16)
            kv_in[h, pl.ds(g * 272 + 256, 16), 128:256] = jnp.zeros((16, 128), BF16)
    r_t = mm(wr_t[...], on[...], NT)
    for n in range(8):
        tile = r_t[:, n * 128 : n * 128 + 128]
        turn[n * 64 : n * 64 + 32, :] = tile
        turn[n * 64 + 32 : n * 64 + 64, :] = pltpu.roll(tile, 64, 1)
    low = iota((16, 128), 1) < 64
    for n in range(16):
        even = turn[pl.ds(2 * n, 16, stride=32), :]
        odd = turn[pl.ds(2 * n + 1, 16, stride=32), :]
        right_in[:, n * 128 : n * 128 + 128] = jnp.where(low, even, pltpu.roll(odd, 64, 1)).astype(BF16)
    right_in[:, 2048:2176] = live_b
    four = jnp.concatenate([wl_t[...]] * 4, axis=0)
    l_all = mm(on[...], four, NT)
    l_all = jnp.where(iota((1024, 128), 0) % 4 == iota((1024, 128), 1) // 32, l_all, 0.0).astype(BF16)
    to, fro = iota((256, 1024), 0), iota((256, 1024), 1)
    pick = ((fro // 64 == to % 16) & ((fro % 64) // 4 == to // 16)).astype(F32).astype(BF16)
    l_rows = mm(pick, l_all).astype(BF16)
    for n in range(16):
        left_in[:, n * 128 : n * 128 + 128] = l_rows[n * 16 : n * 16 + 16]
    left_in[:, 2048:2176] = live_b

    @pl.when(q != r)
    def _():
        pl.semaphore_wait(barrier, 19)

    @pl.when(q == r)
    def _():
        pl.semaphore_wait(barrier, 18)

    def rows16(ref, at):
        return ref.at[pl.ds(pl.multiple_of(at * 16, 16), 16), :]

    own_q = pl.ds(pl.multiple_of(q * 16, 16), 16)
    sends = []

    def go(c):
        c.start()
        sends.append(c)

    trans = rcopy(right_in, rows16(rg, r), t_sem.at[0], t_sem.at[1], dev(r, q))

    @pl.when(q != r)
    def _():
        trans.start()

    @pl.when(q == r)
    def _():
        rg[own_q, :] = right_in[...]

    def ring_from(d, k):
        return (z + NZ - 1 - k) % NZ if d == 0 else (z + 1 + k) % NZ

    def ring_to(d, k):
        return (z + NZ - k) % NZ if d == 0 else (z + k) % NZ

    def ring_dev(d):
        return dev(up_q if d == 0 else down_q, r)

    def side(a):
        return x_hi if a == 0 else 1 - x_hi

    def kv_copy(zo, g, a, d, k):
        ref = kvg.at[zo * 2 + side(a), pl.ds(g * 272, 272), :]
        n = g * 16 + a * 8 + d * 4 + k
        return rcopy(ref, ref, k_send.at[n], k_recv.at[n], ring_dev(d))

    waiting = [[], []]

    def kv_start(g, a):
        for d in range(2):
            go(kv_copy(ring_to(d, 0), g, a, d, 0))

    def kv_stage(g, a, k):
        for d in range(2):
            if k - 1 < HOPS[a][d]:
                kv_copy(ring_from(d, k - 1), g, a, d, k - 1).wait_recv()
                waiting[g].append(ring_from(d, k - 1) * 2 + side(a))
                if k < HOPS[a][d]:
                    go(kv_copy(ring_to(d, k), g, a, d, k))

    def right_copy(zo, d, k):
        ref = rows16(rg, zo * 2 + x_hi)
        return rcopy(ref, ref, r_send.at[d * 4 + k], r_recv.at[d * 4 + k], ring_dev(d))

    def mate_copy(zo, n, u):
        ref = rows16(rg, zo * 2 + u)
        return rcopy(ref, ref, rx_send.at[n], rx_recv.at[n], dev(mate_q, r))

    def right_stage(k):
        for d in range(2):
            if k - 1 < HOPS[0][d]:
                zo = ring_from(d, k - 1)
                right_copy(zo, d, k - 1).wait_recv()
                if k < HOPS[0][d]:
                    go(right_copy(zo, d, k))
                go(mate_copy(zo, d * 4 + k, x_hi))

    def kx_copy(g):
        at = pl.ds(g * 272, 272)
        return rcopy(kv_in.at[1 - x_hi, at, :], kvg.at[q, at, :], kx_sem.at[2 * g], kx_sem.at[2 * g + 1], dev(mate_q, r))

    def kx_wait(g):
        at = pl.ds(g * 272, 272)
        rcopy(kv_in.at[0, at, :], kvg.at[mate_q, at, :], kx_sem.at[2 * g], kx_sem.at[2 * g + 1], dev(mate_q, r)).wait_recv()
        waiting[g].append(mate_q)

    def left_copy(d):
        return rcopy(left_in, rows16(lg, r), l_send.at[d], l_recv.at[d], dev(q, (r + 2 * d) % 16))

    def left_pass(d, rr):
        ref = rows16(lg, rr)
        return rcopy(ref, ref, l_send.at[8 + d], l_recv.at[8 + d], dev(q, sib_r))

    kvg[q] = kv_in[x_hi]
    kv_start(0, 0)
    lg[pl.ds(pl.multiple_of(r * 16, 16), 16), :] = left_in[...]
    for d in range(1, 8):
        go(left_copy(d))
    go(left_pass(0, r))
    go(kx_copy(0))
    go(kx_copy(1))

    def fill(e, carry):
        blk = w_f32[pl.ds(e, 32, stride=32), :].astype(BF16)
        none = jnp.zeros_like(blk)
        for i in range(4):
            bd[pl.ds(pl.multiple_of(e * 128 + i * 32, 32), 32), :] = jnp.concatenate(
                [blk if i == n else none for n in range(4)], axis=1
            )
        return carry

    @pl.when(q != r)
    def _():
        rcopy(right_in, rows16(rg, q), t_sem.at[0], t_sem.at[1], dev(r, q)).wait_recv()

    for d in range(2):
        go(right_copy(z, d, 0))
    go(mate_copy(z, 0, x_hi))
    loads[0].wait()
    w_f32[...] = w_bf[...].astype(F32)
    lax.fori_loop(0, 32, fill, 0)
    expand[...] = (iota((512, 64), 0) // 8 == iota((512, 64), 1)).astype(F32).astype(BF16)
    head_mask[...] = (iota((512, 256), 0) % 8 == iota((512, 256), 1) // 32).astype(F32)
    loads[1].wait()
    loads[2].wait()
    waiting[0].append(q)
    waiting[1].append(q)
    kx_wait(0)
    kv_start(0, 1)

    def kv_proj(slot, g):
        at = pl.ds(pl.multiple_of(slot * 64, 64), 64)
        block = kvg[slot, pl.ds(g * 272, 256), :]
        keys = mm(block, wk[...]).astype(BF16)
        values = mm(block, wv[...]).astype(BF16)
        for s in range(4):
            kb[g * 4 + s, at, :] = keys[s * 64 : s * 64 + 64]
            vb[g * 4 + s, at, :] = values[s * 64 : s * 64 + 64]

    def flush(g):
        for slot in waiting[g]:
            kv_proj(slot, g)
        waiting[g].clear()

    right_stage(1)
    kv_stage(0, 0, 1)
    flush(0)
    right_stage(2)
    for d in range(1, 8):
        rcopy(left_in, rows16(lg, (r + 16 - 2 * d) % 16), l_send.at[d], l_recv.at[d], dev(q, sib_r)).wait_recv()
        go(left_pass(d, (r + 16 - 2 * d) % 16))
    kv_stage(0, 1, 1)
    right_stage(3)
    kv_stage(0, 0, 2)
    right_stage(4)
    for d in range(8):
        left_pass(d, (sib_r + 16 - 2 * d) % 16).wait_recv()
    kv_stage(0, 1, 2)
    mate_copy(z, 0, 1 - x_hi).wait_recv()
    for d in range(2):
        for k in range(HOPS[0][d]):
            mate_copy(ring_from(d, k), d * 4 + k + 1, 1 - x_hi).wait_recv()
    kv_stage(0, 0, 3)
    kx_wait(1)
    kv_start(1, 0)
    loads[3].wait()

    counts = lax.dot_general(rg[:, 2048:2176], lg[:, 2048:2176], (((0,), (0,)), ((), ())), preferred_element_type=F32)
    inv_c[...] = 1.0 / jnp.maximum(counts[0:64], 1.0)
    for n in range(16):
        rt[n * 128 : n * 128 + 128, :] = rg[:, n * 128 : n * 128 + 128].T
    lane = lax.broadcasted_iota(jnp.int32, (64, 128), 1)
    lane8 = lax.broadcasted_iota(jnp.int32, (8, 128), 1)
    own_half = lane8 // 64 == core
    first = core == 0

    def outer_block(t, carry):
        ib = t // 2 + 2 * ((core + 1 + t) % 2)
        l_blk = lg[:, pl.ds(pl.multiple_of(ib * 512, 512), 512)]
        for ec in range(4):
            o = mm(rt[ec * 512 : ec * 512 + 512, :], l_blk).astype(BF16)
            for e in range(8):
                for g in range(4):
                    at = (ec * 8 + e) * 128
                    osc[g * 64 : g * 64 + 64, at : at + 128] = o[e * 64 : e * 64 + 64, g * 128 : g * 128 + 128]
        res = mm(osc[...], bd[...])
        for g in range(4):
            norms = []
            for n in range(4):
                i = ib * 16 + g * 4 + n
                scale = jnp.sum(jnp.where(lane == i, inv_c[...], 0.0), axis=1, keepdims=True)
                val = pair_in[i] + res[g * 64 : g * 64 + 64, n * 128 : n * 128 + 128] * scale
                pair_out[i] = val
                cen = val - jnp.mean(val, -1, keepdims=True)
                spread = jnp.mean(cen * cen, -1, keepdims=True)
                norms.append((cen * lax.rsqrt(spread + EPSILON) * p_gain[...]).astype(BF16))
            b_t = mm(wb_t[...], jnp.concatenate(norms, axis=0), NT)
            tiles = []
            for n in range(2):
                tile = b_t[0:8, n * 128 : n * 128 + 128]
                turned = pltpu.roll(tile, 64, 1)
                tiles.append(jnp.where(own_half, jnp.where(first, tile, turned), 0.0))
                tiles.append(jnp.where(own_half, jnp.where(first, turned, tile), 0.0))
            bias_own[pl.ds(pl.multiple_of(ib * 128 + g * 32, 32), 32), :] = jnp.concatenate(tiles, axis=0).astype(BF16)
        return carry

    def quarter(c, own):
        return pl.ds(pl.multiple_of((2 * (core if own else 1 - core) + c) * 128, 128), 128)

    def tab(xx, yy, c, own):
        return bias_tab.at[xx // 2, (xx % 2) * 4 + yy, quarter(c, own), :]

    def spread_bias(c):
        at = pl.ds(c * 128, 128)
        rcopy(bias_own.at[quarter(c, False), :], bias_sib.at[at, :], b_sem.at[2 * c], b_sem.at[2 * c + 1], dev(q, sib_r)).wait_recv()
        bias_tab[x_hi, kt, quarter(c, True), :] = bias_own[quarter(c, True), :] + bias_sib[at, :]
        own = tab(x, y, c, True)
        for d in range(1, 16):
            xx, yy = (x + d // 4) % 4, (y + d % 4) % 4
            where = dev(z * 2 + xx // 2, (xx % 2) * 8 + yy * 2 + core)
            go(rcopy(own, own, pl_send.at[c * 16 + d], pl_recv.at[c * 16 + d], where))
        go(rcopy(own, own, f_send.at[c * 16], f_recv.at[c * 16], dev(q, sib_r)))

    def pass_bias(c):
        for d in range(1, 16):
            got = tab((x + 4 - d // 4) % 4, (y + 4 - d % 4) % 4, c, True)
            rcopy(got, got, pl_send.at[c * 16 + d], pl_recv.at[c * 16 + d], dev(q, sib_r)).wait_recv()
            go(rcopy(got, got, f_send.at[c * 16 + d], f_recv.at[c * 16 + d], dev(q, sib_r)))

    for c in range(2):
        lax.fori_loop(2 * c, 2 * c + 1, outer_block, 0)
        at = pl.ds(c * 128, 128)
        go(rcopy(bias_own.at[quarter(c, False), :], bias_sib.at[at, :], b_sem.at[2 * c], b_sem.at[2 * c + 1], dev(q, sib_r)))
        lax.fori_loop(2 * c + 1, 2 * c + 2, outer_block, 0)
        spread_bias(c)
        if c == 0:
            kv_stage(0, 1, 3)
            kv_start(1, 1)
            kv_stage(0, 0, 4)
            kv_stage(0, 1, 4)
            kv_stage(1, 0, 1)
    pair_back = pltpu.make_async_copy(pair_out, pair_hbm_out, in_sem.at[9])
    pair_back.start()
    kv_stage(1, 1, 1)
    flush(0)
    pass_bias(0)
    kv_stage(1, 0, 2)
    pass_bias(1)
    kv_stage(1, 1, 2)
    for c in range(2):
        for d in range(16):
            got = tab((x + 4 - d // 4) % 4, (y + 4 - d % 4) % 4, c, False)
            rcopy(got, got, f_send.at[c * 16 + d], f_recv.at[c * 16 + d], dev(q, sib_r)).wait_recv()

    for n in range(8):
        live = kvg[2 * n, pl.ds(256, 16), 0:128].astype(F32) + kvg[2 * n + 1, pl.ds(256, 16), 0:128].astype(F32)
        mask_tab[:, n * 128 : n * 128 + 128] = jnp.where(live > 0.5, 0.0, MASKED)

    lane_head = lax.broadcasted_iota(jnp.int32, (64, 128), 1) // 32

    def by_head(ref, tile):
        out = ref[pl.ds(tile * 4, 64, stride=8), :]
        for h in range(1, 4):
            out = jnp.where(lane_head == h, ref[pl.ds(tile * 4 + h, 64, stride=8), :], out)
        return out

    for c in loads[4:]:
        c.wait()

    def attend(v, g, dest):
        def rows_of(s):
            return pl.ds(pl.multiple_of(s * 64, 64), 64)

        def cells(s):
            return kvg[z * 2 + v, pl.ds(pl.multiple_of(s * 64 + g * 16, 16), 64), :]

        def look(s, slot):
            queries = (mm(cells(s), wq[...]) * 32**-0.5).astype(BF16)
            spread_q = (mm(expand[...], queries) * head_mask[...]).astype(BF16)
            sc_buf[slot] = mm(spread_q, kb[s], NT)

        def weigh(s, slot):
            m_row = mask_tab[pl.ds(s, 1), :]
            for rb in range(16):
                rows = pl.ds(rb * 32, 32)
                bias = jnp.concatenate([bias_tab[v, n, rows, :].astype(F32) for n in range(8)], axis=1)
                sc = sc_buf[slot, rows, :] + bias + m_row
                w = jnp.exp(sc - jnp.max(sc, -1, keepdims=True))
                tot_buf[slot, rows, :] = jnp.broadcast_to(jnp.sum(w, -1, keepdims=True), (32, 128))
                p_buf[slot, rows, :] = w.astype(BF16)

        def mix(s, slot):
            gates = jax.nn.sigmoid(mm(cells(s), wg[...]))
            mixed = mm(p_buf[slot], vb[s])
            for tile in range(2):
                r_buf[slot, tile] = mixed[:, tile * 128 : tile * 128 + 128]
                num = by_head(r_buf.at[slot, tile], tile)
                den = by_head(tot_buf.at[slot], tile)
                dest[rows_of(s), pl.ds(tile * 128, 128)] = (
                    num / den * gates[:, tile * 128 : tile * 128 + 128]
                ).astype(BF16)

        def two(n, carry):
            s = n * 2 + g * 4
            look(s + 1, 1)
            weigh(s, 0)
            mix(s, 0)
            weigh(s + 1, 1)
            look(g * 4 + (n * 2 + 2) % 4, 0)
            mix(s + 1, 1)
            return carry

        look(g * 4, 0)
        lax.fori_loop(0, 2, two, 0)

    def finish(gated, which):
        def part(n, carry):
            at = pl.ds(pl.multiple_of(n * 256, 256), 256)
            after = align_in[which, at, :].astype(F32) + mm(gated[at, :], wo[...])
            cen = after - jnp.mean(after, -1, keepdims=True)
            spread = jnp.mean(cen * cen, -1, keepdims=True)
            norm = (cen * lax.rsqrt(spread + EPSILON) * t_gain[...]).astype(BF16)
            hidden = jnp.maximum(mm(norm, w_up[...]), 0.0).astype(BF16)
            align_out[which, at, :] = after + mm(hidden, w_down[...])
            return carry

        lax.fori_loop(0, 2, part, 0)

    def back(g):
        at = pl.ds(g * 256, 256)
        return rcopy(gate_far.at[at, :], gate_in.at[at, :], g_sem.at[2 * g], g_sem.at[2 * g + 1], dev(mate_q, r))

    attend(1 - x_hi, 0, gate_far)
    go(back(0))
    kv_stage(1, 0, 3)
    kv_stage(1, 1, 3)
    flush(1)
    attend(x_hi, 0, gate_own)
    kv_stage(1, 0, 4)
    kv_stage(1, 1, 4)
    flush(1)
    attend(1 - x_hi, 1, gate_far)
    go(back(1))
    attend(x_hi, 1, gate_own)
    finish(gate_own, x_hi)
    for g in range(2):
        back(g).wait_recv()
    finish(gate_in, 1 - x_hi)

    @pl.when(q != r)
    def _():
        trans.wait_send()

    for c in sends:
        c.wait_send()
    pair_back.wait()


def on_device(
    alignment, alignment_mask, residue_mask, pair_input, outer_gain, left_weight, right_weight, outer_weight, pair_gain,
    bias_weight, row_gain, query_weight, key_weight, value_weight, gate_weight, output_weight, transition_gain, up_weight,
    down_weight,
):
    vm = pl.BlockSpec(memory_space=pltpu.VMEM)
    hbm = pl.BlockSpec(memory_space=pl.ANY)
    dma, v = pltpu.SemaphoreType.DMA, pltpu.VMEM
    pair_out, align_out = pl.pallas_call(
        kernel,
        out_shape=(jax.ShapeDtypeStruct((64, 64, 128), F32), jax.ShapeDtypeStruct((2, 512, 256), F32)),
        in_specs=[vm] * 10 + [hbm] * 9,
        out_specs=(hbm, vm),
        scratch_shapes=[
            v((16, 2176), BF16), v((16, 2176), BF16), v((2, 544, 256), BF16), v((1024, 256), BF16), v((16, 128), F32),
            v((512, 128), F32), v((64, 64, 128), F32), v((64, 64, 128), F32), v((1024, 128), BF16), v((1024, 128), F32),
            v((256, 256), BF16), v((256, 256), BF16), v((256, 256), BF16), v((256, 256), BF16), v((256, 256), BF16),
            v((256, 1024), BF16), v((1024, 256), BF16), v((512, 64), BF16), v((512, 256), F32), dma((10,)),
            v((256, 2176), BF16), v((256, 2176), BF16), v((2048, 256), BF16), v((4096, 512), BF16), v((256, 4096), BF16),
            v((64, 128), F32), v((512, 128), BF16), v((256, 128), BF16), v((2, 8, 512, 128), BF16),
            v((16, 544, 256), BF16), v((8, 1024, 256), BF16), v((8, 1024, 256), BF16), v((16, 1024), F32),
            v((2, 512, 1024), F32), v((2, 512, 1024), BF16), v((2, 2, 512, 128), F32), v((2, 512, 128), F32),
            v((512, 256), BF16), v((512, 256), BF16), v((512, 256), BF16),
            dma((16,)), dma((16,)), dma((2,)), dma((8,)), dma((8,)), dma((4,)), dma((8,)), dma((8,)), dma((32,)), dma((32,)),
            dma((4,)), dma((32,)), dma((32,)), dma((32,)), dma((32,)), dma((4,)),
        ],
        compiler_params=pltpu.CompilerParams(collective_id=0, has_side_effects=True, vmem_limit_bytes=60 << 20),
    )(
        alignment.reshape(2, 512, 256), alignment_mask, residue_mask.reshape(8, 128), outer_gain.reshape(1, 256), left_weight.T,
        right_weight.T, pair_gain.reshape(1, 128), bias_weight.T, row_gain.reshape(1, 256), transition_gain.reshape(1, 256),
        pair_input, outer_weight, query_weight, key_weight, value_weight, gate_weight, output_weight, up_weight, down_weight,
    )
    return pair_out, align_out.reshape(16, 64, 256)


def solution(mesh):
    rep = P()
    in_specs = (P("res", "seq", None), P("res", "seq"), rep, P("seq", "res", None)) + (rep,) * 15
    out_specs = (P("seq", "res", None), P("res", "seq", None))
    return jax.shard_map(on_device, mesh=mesh, in_specs=in_specs, out_specs=out_specs, check_vma=False)
```

```python
import functools

import jax
import jax.numpy as jnp
from jax import lax
from jax.experimental import pallas as pl
from jax.experimental.pallas import tpu as pltpu
from jax.sharding import PartitionSpec as P

EPSILON = 1e-05
MASKED = -1000000000.0
MESH = pl.DeviceIdType.MESH
F32, BF16 = jnp.float32, jnp.bfloat16
NN = (((1,), (0,)), ((), ()))
NT = (((1,), (1,)), ((), ()))
NZ = 8
HOPS = ((4, 3), (3, 4))


def mm(a, b, dims=NN):
    return lax.dot_general(a, b, dims, preferred_element_type=F32)


def kernel(
    align_in, a_mask, r_mask, o_gain, wl_t, wr_t, p_gain, wb_t, row_gain, t_gain,
    pair_hbm, ow_hbm, wq_hbm, wk_hbm, wv_hbm, wg_hbm, wo_hbm, up_hbm, down_hbm,
    pair_hbm_out, align_out,
    left_in, right_in, kv_in, on, live_f, turn, pair_in, pair_out, w_bf, w_f32, wq, wk, wv, wg, wo, w_up, w_down,
    expand, head_mask, in_sem,
    lg, rg, rt, bd, osc, inv_c, bias_own, bias_sib, bias_tab, kvg, kb, vb, mask_tab, sc_buf, p_buf, r_buf, tot_buf, top_buf,
    gate_own, gate_far, gate_in,
    l_send, l_recv, t_sem, rx_send, rx_recv, kx_sem, r_send, r_recv, k_send, k_recv, b_sem, pl_send, pl_recv, f_send, f_recv,
    g_sem,
):
    q = lax.axis_index("seq")
    r = lax.axis_index("res")
    z, x_hi = q // 2, q % 2
    core = r % 2
    y = (r // 2) % 4
    x_lo = r // 8
    x = x_hi * 2 + x_lo
    kt = r // 2
    mate_q = q + 1 - 2 * x_hi
    sib_r = r + 1 - 2 * core
    up_q = ((z + 1) % NZ) * 2 + x_hi
    down_q = ((z + NZ - 1) % NZ) * 2 + x_hi

    def dev(qq, rr):
        return {"seq": qq, "res": rr}

    def rcopy(src, dst, ss, rs, where):
        return pltpu.make_async_remote_copy(
            src_ref=src, dst_ref=dst, send_sem=ss, recv_sem=rs, device_id=where, device_id_type=MESH
        )

    barrier = pltpu.get_barrier_semaphore()

    def hello(where):
        pl.semaphore_signal(barrier, inc=1, device_id=where, device_id_type=MESH)

    for d in range(1, 8):
        hello(dev(q, (r + 2 * d) % 16))
    hello(dev(q, sib_r))
    for d in range(8):
        hello(dev(mate_q, (r + 2 * d) % 16))
    hello(dev(up_q, r))
    hello(dev(down_q, r))

    @pl.when(q != r)
    def _():
        hello(dev(r, q))

    loads = [
        pltpu.make_async_copy(src, dst, in_sem.at[n])
        for n, (src, dst) in enumerate(
            (
                (ow_hbm, w_bf), (wk_hbm, wk), (wv_hbm, wv), (pair_hbm, pair_in), (wq_hbm, wq), (wg_hbm, wg), (wo_hbm, wo),
                (up_hbm, w_up), (down_hbm, w_down),
            )
        )
    ]
    for c in loads:
        c.start()

    def iota(shape, dim):
        return lax.broadcasted_iota(jnp.int32, shape, dim)

    flag_row = r_mask[pl.ds(q // 2, 1), :].astype(F32)
    flag_row = jnp.where(x_hi == 0, flag_row, pltpu.roll(flag_row, 64, 1))
    live_f[...] = jnp.zeros_like(live_f)
    live_f[:, 0:64] = a_mask[...].astype(F32) * flag_row[:, 0:64]
    live = live_f[...]
    live_b = live.astype(BF16)

    def norms(n, carry):
        at = pl.ds(pl.multiple_of(n * 256, 256), 256)
        vals = align_in[n // 2, pl.ds(pl.multiple_of((n % 2) * 256, 256), 256), :].astype(F32)
        cen = vals - jnp.mean(vals, -1, keepdims=True)
        spread = jnp.mean(cen * cen, -1, keepdims=True)
        norm = cen * lax.rsqrt(spread + EPSILON)
        pick = (iota((256, 16), 0) // 64 + n * 4 == iota((256, 16), 1)).astype(F32).astype(BF16)
        flags = mm(pick, live_b)
        flag = jnp.sum(jnp.where(iota((256, 128), 0) % 64 == iota((256, 128), 1), flags, 0.0), -1, keepdims=True)
        on[at, :] = (norm * o_gain[...] * flag).astype(BF16)
        kv_in[n // 2, pl.ds(pl.multiple_of((n % 2) * 272, 16), 256), :] = (norm * row_gain[...]).astype(BF16)
        return carry

    lax.fori_loop(0, 4, norms, 0)
    marks = jnp.where(x_hi == 0, live, pltpu.roll(live, 64, 1))
    for h in range(2):
        for g in range(2):
            kv_in[h, pl.ds(g * 272 + 256, 16), 0:128] = jnp.concatenate(
                [marks[h * 8 : h * 8 + 8], jnp.zeros((8, 128), F32)], axis=0
            ).astype(BF16)
            kv_in[h, pl.ds(g * 272 + 256, 16), 128:256] = jnp.zeros((16, 128), BF16)
    r_t = mm(wr_t[...], on[...], NT)
    for n in range(8):
        tile = r_t[:, n * 128 : n * 128 + 128]
        turn[n * 64 : n * 64 + 32, :] = tile
        turn[n * 64 + 32 : n * 64 + 64, :] = pltpu.roll(tile, 64, 1)
    low = iota((16, 128), 1) < 64
    for n in range(16):
        even = turn[pl.ds(2 * n, 16, stride=32), :]
        odd = turn[pl.ds(2 * n + 1, 16, stride=32), :]
        right_in[:, n * 128 : n * 128 + 128] = jnp.where(low, even, pltpu.roll(odd, 64, 1)).astype(BF16)
    right_in[:, 2048:2176] = live_b
    four = jnp.concatenate([wl_t[...]] * 4, axis=0)
    l_all = mm(on[...], four, NT)
    l_all = jnp.where(iota((1024, 128), 0) % 4 == iota((1024, 128), 1) // 32, l_all, 0.0).astype(BF16)
    to, fro = iota((256, 1024), 0), iota((256, 1024), 1)
    pick = ((fro // 64 == to % 16) & ((fro % 64) // 4 == to // 16)).astype(F32).astype(BF16)
    l_rows = mm(pick, l_all).astype(BF16)
    for n in range(16):
        left_in[:, n * 128 : n * 128 + 128] = l_rows[n * 16 : n * 16 + 16]
    left_in[:, 2048:2176] = live_b

    @pl.when(q != r)
    def _():
        pl.semaphore_wait(barrier, 19)

    @pl.when(q == r)
    def _():
        pl.semaphore_wait(barrier, 18)

    def rows16(ref, at):
        return ref.at[pl.ds(pl.multiple_of(at * 16, 16), 16), :]

    own_q = pl.ds(pl.multiple_of(q * 16, 16), 16)
    sends = []

    def go(c):
        c.start()
        sends.append(c)

    trans = rcopy(right_in, rows16(rg, r), t_sem.at[0], t_sem.at[1], dev(r, q))

    @pl.when(q != r)
    def _():
        trans.start()

    @pl.when(q == r)
    def _():
        rg[own_q, :] = right_in[...]

    def ring_from(d, k):
        return (z + NZ - 1 - k) % NZ if d == 0 else (z + 1 + k) % NZ

    def ring_to(d, k):
        return (z + NZ - k) % NZ if d == 0 else (z + k) % NZ

    def ring_dev(d):
        return dev(up_q if d == 0 else down_q, r)

    def side(a):
        return x_hi if a == 0 else 1 - x_hi

    def kv_copy(zo, g, a, d, k):
        ref = kvg.at[zo * 2 + side(a), pl.ds(g * 272, 272), :]
        n = g * 16 + a * 8 + d * 4 + k
        return rcopy(ref, ref, k_send.at[n], k_recv.at[n], ring_dev(d))

    waiting = [[], []]

    def kv_start(g, a):
        for d in range(2):
            go(kv_copy(ring_to(d, 0), g, a, d, 0))

    def kv_stage(g, a, k):
        for d in range(2):
            if k - 1 < HOPS[a][d]:
                kv_copy(ring_from(d, k - 1), g, a, d, k - 1).wait_recv()
                waiting[g].append(ring_from(d, k - 1) * 2 + side(a))
                if k < HOPS[a][d]:
                    go(kv_copy(ring_to(d, k), g, a, d, k))

    def right_copy(zo, d, k):
        ref = rows16(rg, zo * 2 + x_hi)
        return rcopy(ref, ref, r_send.at[d * 4 + k], r_recv.at[d * 4 + k], ring_dev(d))

    def mate_copy(zo, n, u):
        ref = rows16(rg, zo * 2 + u)
        return rcopy(ref, ref, rx_send.at[n], rx_recv.at[n], dev(mate_q, r))

    def right_stage(k):
        for d in range(2):
            if k - 1 < HOPS[0][d]:
                zo = ring_from(d, k - 1)
                right_copy(zo, d, k - 1).wait_recv()
                if k < HOPS[0][d]:
                    go(right_copy(zo, d, k))
                go(mate_copy(zo, d * 4 + k, x_hi))

    def kx_copy(g):
        at = pl.ds(g * 272, 272)
        return rcopy(kv_in.at[1 - x_hi, at, :], kvg.at[q, at, :], kx_sem.at[2 * g], kx_sem.at[2 * g + 1], dev(mate_q, r))

    def kx_wait(g):
        at = pl.ds(g * 272, 272)
        rcopy(kv_in.at[0, at, :], kvg.at[mate_q, at, :], kx_sem.at[2 * g], kx_sem.at[2 * g + 1], dev(mate_q, r)).wait_recv()
        waiting[g].append(mate_q)

    def left_copy(d):
        return rcopy(left_in, rows16(lg, r), l_send.at[d], l_recv.at[d], dev(q, (r + 2 * d) % 16))

    def left_pass(d, rr):
        ref = rows16(lg, rr)
        return rcopy(ref, ref, l_send.at[8 + d], l_recv.at[8 + d], dev(q, sib_r))

    kvg[q] = kv_in[x_hi]
    kv_start(0, 0)
    lg[pl.ds(pl.multiple_of(r * 16, 16), 16), :] = left_in[...]
    for d in range(1, 8):
        go(left_copy(d))
    go(left_pass(0, r))
    go(kx_copy(0))

    def fill(e, carry):
        blk = w_f32[pl.ds(e, 32, stride=32), :].astype(BF16)
        none = jnp.zeros_like(blk)
        for i in range(4):
            bd[pl.ds(pl.multiple_of(e * 128 + i * 32, 32), 32), :] = jnp.concatenate(
                [blk if i == n else none for n in range(4)], axis=1
            )
        return carry

    @pl.when(q != r)
    def _():
        rcopy(right_in, rows16(rg, q), t_sem.at[0], t_sem.at[1], dev(r, q)).wait_recv()

    for d in range(2):
        go(right_copy(z, d, 0))
    go(mate_copy(z, 0, x_hi))
    loads[0].wait()
    w_f32[...] = w_bf[...].astype(F32)
    lax.fori_loop(0, 32, fill, 0)
    expand[...] = (iota((512, 64), 0) // 8 == iota((512, 64), 1)).astype(F32).astype(BF16)
    head_mask[...] = (iota((512, 256), 0) % 8 == iota((512, 256), 1) // 32).astype(F32)
    loads[1].wait()
    loads[2].wait()
    waiting[0].append(q)
    waiting[1].append(q)
    kx_wait(0)
    kv_start(0, 1)

    def kv_proj(slot, g):
        at = pl.ds(pl.multiple_of(slot * 64, 64), 64)
        block = kvg[slot, pl.ds(g * 272, 256), :]
        keys = mm(block, wk[...]).astype(BF16)
        values = mm(block, wv[...]).astype(BF16)
        for s in range(4):
            kb[g * 4 + s, at, :] = keys[s * 64 : s * 64 + 64]
            vb[g * 4 + s, at, :] = values[s * 64 : s * 64 + 64]

    def flush(g):
        for slot in waiting[g]:
            kv_proj(slot, g)
        waiting[g].clear()

    right_stage(1)
    kv_stage(0, 0, 1)
    go(kx_copy(1))
    right_stage(2)
    kv_stage(0, 1, 1)
    right_stage(3)
    for d in range(1, 8):
        rcopy(left_in, rows16(lg, (r + 16 - 2 * d) % 16), l_send.at[d], l_recv.at[d], dev(q, sib_r)).wait_recv()
        go(left_pass(d, (r + 16 - 2 * d) % 16))
    kv_stage(0, 0, 2)
    right_stage(4)
    kv_start(1, 0)
    for d in range(8):
        left_pass(d, (sib_r + 16 - 2 * d) % 16).wait_recv()
    mate_copy(z, 0, 1 - x_hi).wait_recv()
    for d in range(2):
        for k in range(HOPS[0][d]):
            mate_copy(ring_from(d, k), d * 4 + k + 1, 1 - x_hi).wait_recv()
    kv_stage(0, 1, 2)
    kx_wait(1)
    kv_start(1, 1)
    loads[3].wait()

    counts = lax.dot_general(rg[:, 2048:2176], lg[:, 2048:2176], (((0,), (0,)), ((), ())), preferred_element_type=F32)
    inv_c[...] = 1.0 / jnp.maximum(counts[0:64], 1.0)
    for n in range(16):
        rt[n * 128 : n * 128 + 128, :] = rg[:, n * 128 : n * 128 + 128].T
    lane = lax.broadcasted_iota(jnp.int32, (64, 128), 1)
    lane8 = lax.broadcasted_iota(jnp.int32, (8, 128), 1)
    own_half = lane8 // 64 == core
    first = core == 0

    def outer_block(t, carry):
        ib = t // 2 + 2 * ((core + 1 + t) % 2)
        l_blk = lg[:, pl.ds(pl.multiple_of(ib * 512, 512), 512)]
        for ec in range(4):
            o = mm(rt[ec * 512 : ec * 512 + 512, :], l_blk).astype(BF16)
            for e in range(8):
                for g in range(4):
                    at = (ec * 8 + e) * 128
                    osc[g * 64 : g * 64 + 64, at : at + 128] = o[e * 64 : e * 64 + 64, g * 128 : g * 128 + 128]
        res = mm(osc[...], bd[...])
        for g in range(4):
            norms = []
            for n in range(4):
                i = ib * 16 + g * 4 + n
                scale = jnp.sum(jnp.where(lane == i, inv_c[...], 0.0), axis=1, keepdims=True)
                update = res[g * 64 : g * 64 + 64, n * 128 : n * 128 + 128] * scale
                pair_out[i] = update
                val = pair_in[i] + update
                cen = val - jnp.mean(val, -1, keepdims=True)
                spread = jnp.mean(cen * cen, -1, keepdims=True)
                norms.append((cen * lax.rsqrt(spread + EPSILON) * p_gain[...]).astype(BF16))
            b_t = mm(wb_t[...], jnp.concatenate(norms, axis=0), NT)
            tiles = []
            for n in range(2):
                tile = b_t[0:8, n * 128 : n * 128 + 128]
                turned = pltpu.roll(tile, 64, 1)
                tiles.append(jnp.where(own_half, jnp.where(first, tile, turned), 0.0))
                tiles.append(jnp.where(own_half, jnp.where(first, turned, tile), 0.0))
            bias_own[pl.ds(pl.multiple_of(ib * 128 + g * 32, 32), 32), :] = jnp.concatenate(tiles, axis=0).astype(BF16)
        return carry

    def quarter(c, own):
        return pl.ds(pl.multiple_of((2 * (core if own else 1 - core) + c) * 128, 128), 128)

    def tab(xx, yy, c, own):
        return bias_tab.at[xx // 2, (xx % 2) * 4 + yy, quarter(c, own), :]

    def spread_bias(c):
        at = pl.ds(c * 128, 128)
        rcopy(bias_own.at[quarter(c, False), :], bias_sib.at[at, :], b_sem.at[2 * c], b_sem.at[2 * c + 1], dev(q, sib_r)).wait_recv()
        bias_tab[x_hi, kt, quarter(c, True), :] = bias_own[quarter(c, True), :] + bias_sib[at, :]
        own = tab(x, y, c, True)
        for d in range(1, 16):
            xx, yy = (x + d // 4) % 4, (y + d % 4) % 4
            where = dev(z * 2 + xx // 2, (xx % 2) * 8 + yy * 2 + core)
            go(rcopy(own, own, pl_send.at[c * 16 + d], pl_recv.at[c * 16 + d], where))
        go(rcopy(own, own, f_send.at[c * 16], f_recv.at[c * 16], dev(q, sib_r)))

    def pass_bias(c):
        for d in range(1, 16):
            got = tab((x + 4 - d // 4) % 4, (y + 4 - d % 4) % 4, c, True)
            rcopy(got, got, pl_send.at[c * 16 + d], pl_recv.at[c * 16 + d], dev(q, sib_r)).wait_recv()
            go(rcopy(got, got, f_send.at[c * 16 + d], f_recv.at[c * 16 + d], dev(q, sib_r)))

    for c in range(2):
        lax.fori_loop(2 * c, 2 * c + 1, outer_block, 0)
        at = pl.ds(c * 128, 128)
        go(rcopy(bias_own.at[quarter(c, False), :], bias_sib.at[at, :], b_sem.at[2 * c], b_sem.at[2 * c + 1], dev(q, sib_r)))
        lax.fori_loop(2 * c + 1, 2 * c + 2, outer_block, 0)
        spread_bias(c)
        if c == 0:
            kv_stage(0, 0, 3)
            kv_stage(1, 0, 1)
    pair_back = pltpu.make_async_copy(pair_out, pair_hbm_out, in_sem.at[9])
    pair_back.start()
    kv_stage(0, 1, 3)
    kv_stage(1, 1, 1)
    pass_bias(0)
    kv_stage(1, 0, 2)
    kv_stage(0, 0, 4)
    flush(0)
    kv_stage(1, 1, 2)
    pass_bias(1)
    kv_stage(0, 1, 4)
    flush(0)
    for c in range(2):
        for d in range(16):
            got = tab((x + 4 - d // 4) % 4, (y + 4 - d % 4) % 4, c, False)
            rcopy(got, got, f_send.at[c * 16 + d], f_recv.at[c * 16 + d], dev(q, sib_r)).wait_recv()

    for n in range(8):
        live = kvg[2 * n, pl.ds(256, 16), 0:128].astype(F32) + kvg[2 * n + 1, pl.ds(256, 16), 0:128].astype(F32)
        mask_tab[:, n * 128 : n * 128 + 128] = jnp.where(live > 0.5, 0.0, MASKED)

    lane_head = lax.broadcasted_iota(jnp.int32, (64, 128), 1) // 32

    def by_head(ref, tile):
        out = ref[pl.ds(tile * 4, 64, stride=8), :]
        for h in range(1, 4):
            out = jnp.where(lane_head == h, ref[pl.ds(tile * 4 + h, 64, stride=8), :], out)
        return out

    for c in loads[4:]:
        c.wait()

    def attend(v, g, dest):
        def rows_of(s):
            return pl.ds(pl.multiple_of(s * 64, 64), 64)

        def cells(s):
            return kvg[z * 2 + v, pl.ds(pl.multiple_of(s * 64 + g * 16, 16), 64), :]

        def look(s, slot):
            queries = (mm(cells(s), wq[...]) * 32**-0.5).astype(BF16)
            spread_q = (mm(expand[...], queries) * head_mask[...]).astype(BF16)
            sc = mm(spread_q, kb[s], NT)
            m_row = mask_tab[pl.ds(s, 1), :]
            for rb in range(16):
                rows = pl.ds(rb * 32, 32)
                top = None
                for n in range(8):
                    part = sc[rb * 32 : rb * 32 + 32, n * 128 : n * 128 + 128] + bias_tab[v, n, rows, :].astype(F32)
                    part = part + m_row[:, n * 128 : n * 128 + 128]
                    sc_buf[slot, rows, n * 128 : n * 128 + 128] = part
                    top = part if n == 0 else jnp.maximum(top, part)
                top_buf[slot, rows, :] = jnp.broadcast_to(jnp.max(top, -1, keepdims=True), (32, 128))

        def weigh(slot):
            for rb in range(16):
                rows = pl.ds(rb * 32, 32)
                top = top_buf[slot, rows, :]
                total = None
                for n in range(8):
                    w = jnp.exp(sc_buf[slot, rows, n * 128 : n * 128 + 128] - top)
                    p_buf[slot, rows, n * 128 : n * 128 + 128] = w.astype(BF16)
                    total = w if n == 0 else total + w
                tot_buf[slot, rows, :] = jnp.broadcast_to(jnp.sum(total, -1, keepdims=True), (32, 128))

        def mix(s, slot):
            gates = jax.nn.sigmoid(mm(cells(s), wg[...]))
            mixed = mm(p_buf[slot], vb[s])
            for tile in range(2):
                r_buf[slot, tile] = mixed[:, tile * 128 : tile * 128 + 128]
                num = by_head(r_buf.at[slot, tile], tile)
                den = by_head(tot_buf.at[slot], tile)
                dest[rows_of(s), pl.ds(tile * 128, 128)] = (
                    num / den * gates[:, tile * 128 : tile * 128 + 128]
                ).astype(BF16)

        def two(n, carry):
            s = n * 2 + g * 4
            look(s + 1, 1)
            weigh(0)
            mix(s, 0)
            weigh(1)
            look(g * 4 + (n * 2 + 2) % 4, 0)
            mix(s + 1, 1)
            return carry

        look(g * 4, 0)
        lax.fori_loop(0, 2, two, 0)

    def finish(gated, which):
        def part(n, carry):
            at = pl.ds(pl.multiple_of(n * 256, 256), 256)
            after = align_in[which, at, :].astype(F32) + mm(gated[at, :], wo[...])
            cen = after - jnp.mean(after, -1, keepdims=True)
            spread = jnp.mean(cen * cen, -1, keepdims=True)
            norm = (cen * lax.rsqrt(spread + EPSILON) * t_gain[...]).astype(BF16)
            hidden = jnp.maximum(mm(norm, w_up[...]), 0.0).astype(BF16)
            align_out[which, at, :] = after + mm(hidden, w_down[...])
            return carry

        lax.fori_loop(0, 2, part, 0)

    def back(g):
        at = pl.ds(g * 256, 256)
        return rcopy(gate_far.at[at, :], gate_in.at[at, :], g_sem.at[2 * g], g_sem.at[2 * g + 1], dev(mate_q, r))

    attend(1 - x_hi, 0, gate_far)
    go(back(0))
    kv_stage(1, 0, 3)
    kv_stage(1, 1, 3)
    flush(1)
    attend(x_hi, 0, gate_own)
    kv_stage(1, 0, 4)
    kv_stage(1, 1, 4)
    flush(1)
    attend(1 - x_hi, 1, gate_far)
    go(back(1))
    attend(x_hi, 1, gate_own)
    finish(gate_own, x_hi)
    for g in range(2):
        back(g).wait_recv()
    finish(gate_in, 1 - x_hi)

    @pl.when(q != r)
    def _():
        trans.wait_send()

    for c in sends:
        c.wait_send()
    pair_back.wait()


def on_device(
    alignment, alignment_mask, residue_mask, pair_input, outer_gain, left_weight, right_weight, outer_weight, pair_gain,
    bias_weight, row_gain, query_weight, key_weight, value_weight, gate_weight, output_weight, transition_gain, up_weight,
    down_weight,
):
    vm = pl.BlockSpec(memory_space=pltpu.VMEM)
    hbm = pl.BlockSpec(memory_space=pl.ANY)
    dma, v = pltpu.SemaphoreType.DMA, pltpu.VMEM
    pair_out, align_out = pl.pallas_call(
        kernel,
        out_shape=(jax.ShapeDtypeStruct((64, 64, 128), F32), jax.ShapeDtypeStruct((2, 512, 256), F32)),
        in_specs=[vm] * 10 + [hbm] * 9,
        out_specs=(hbm, vm),
        scratch_shapes=[
            v((16, 2176), BF16), v((16, 2176), BF16), v((2, 544, 256), BF16), v((1024, 256), BF16), v((16, 128), F32),
            v((512, 128), F32), v((64, 64, 128), F32), v((64, 64, 128), F32), v((1024, 128), BF16), v((1024, 128), F32),
            v((256, 256), BF16), v((256, 256), BF16), v((256, 256), BF16), v((256, 256), BF16), v((256, 256), BF16),
            v((256, 1024), BF16), v((1024, 256), BF16), v((512, 64), BF16), v((512, 256), F32), dma((10,)),
            v((256, 2176), BF16), v((256, 2176), BF16), v((2048, 256), BF16), v((4096, 512), BF16), v((256, 4096), BF16),
            v((64, 128), F32), v((512, 128), BF16), v((256, 128), BF16), v((2, 8, 512, 128), BF16),
            v((16, 544, 256), BF16), v((8, 1024, 256), BF16), v((8, 1024, 256), BF16), v((16, 1024), F32),
            v((2, 512, 1024), F32), v((2, 512, 1024), BF16), v((2, 2, 512, 128), F32), v((2, 512, 128), F32),
            v((2, 512, 128), F32),
            v((512, 256), BF16), v((512, 256), BF16), v((512, 256), BF16),
            dma((16,)), dma((16,)), dma((2,)), dma((8,)), dma((8,)), dma((4,)), dma((8,)), dma((8,)), dma((32,)), dma((32,)),
            dma((4,)), dma((32,)), dma((32,)), dma((32,)), dma((32,)), dma((4,)),
        ],
        compiler_params=pltpu.CompilerParams(collective_id=0, has_side_effects=True, vmem_limit_bytes=60 << 20),
    )(
        alignment.reshape(2, 512, 256), alignment_mask, residue_mask.reshape(8, 128), outer_gain.reshape(1, 256), left_weight.T,
        right_weight.T, pair_gain.reshape(1, 128), bias_weight.T, row_gain.reshape(1, 256), transition_gain.reshape(1, 256),
        pair_input, outer_weight, query_weight, key_weight, value_weight, gate_weight, output_weight, up_weight, down_weight,
    )
    return pair_input + pair_out, align_out.reshape(16, 64, 256)


def solution(mesh):
    rep = P()
    in_specs = (P("res", "seq", None), P("res", "seq"), rep, P("seq", "res", None)) + (rep,) * 15
    out_specs = (P("seq", "res", None), P("res", "seq", None))
    return jax.shard_map(on_device, mesh=mesh, in_specs=in_specs, out_specs=out_specs, check_vma=False)
```
